32 devices in a mesh: dom: 8 (over z, x), attr: 4 (over y, core).
Axes of the slice: x: 2, y: 2, z: 4, core: 2. Of those that a mesh axis runs over, the one named last changes fastest.
Arguments:
- records: bfloat16 [12288, 1024], P('dom', 'attr'), may hold values from -6 to 6
- owner: int32 [12288, 1], P('dom'), may hold values from 0 to 7; in each aligned block of 1536 rows (0 to 1535, 1536 to 3071, ...) at most 384 rows name the same one
- entity_means: bfloat16 [4096, 1024], P('dom', 'attr'), may hold values from -6 to 6
- noise_bits: int32 [24576, 512], P('dom'), may hold values from 0 to 8191
Outputs:
- new_means: float32 [4096, 1024], P('dom', 'attr')
- gram: float32 [1024, 1024], P(('dom', 'attr'))
The draws below stay inside these ranges and needn't reach their ends.
Inputs may be any that keep to these rules, and one draw needn't show every extreme that they name: `owner`: among the records of one index of dom at most 384 name the same partition, and in every draw some partition is named by exactly 384 of them.
All inputs are finite; a program needn't handle non-finite values.
Results may differ from the reference program's by a relative error of at most 0.0013.
Values may be sent and summed in bfloat16 or wider, within the bound.
A program may use at most 64 MiB of HBM per device.

```python
import math
import jax
import jax.numpy as jnp
import numpy as np
from jax import lax

E = 1024
ENT_DEV = 512
R_DEV = 1536
CAP = 384
SLOTS = 3072
RECORDS = 12288
ENTITIES = 4096
N_DOM = 8


def touch_ends(array, rng, smallest, largest):
    place = [jax.random.randint(jax.random.fold_in(rng, axis), (), 0, length) for axis, length in enumerate(array.shape)]
    main_axis = array.shape.index(max(array.shape))
    next_to = place[:main_axis] + [(place[main_axis] + 1) % array.shape[main_axis]] + place[main_axis + 1:]
    return array.at[tuple(place)].set(smallest).at[tuple(next_to)].set(largest)


def strengthened(drawn, own_key, source, target, blocks, factor):
    owner, partner = [(jnp.arange(drawn.shape[dim]) // (drawn.shape[dim] // blocks)).reshape([-1 if axis == dim else 1 for axis in range(drawn.ndim)]) for dim in (source, target)]
    chosen = jax.random.permutation(own_key, blocks)[partner]
    strong = (owner == chosen) | (owner == (partner + blocks // 2) % blocks)
    return jnp.where(strong, factor * drawn, drawn)


def level_of(rng, shape, pieces, low, high):
    loudness, own = 1.0, jax.random.fold_in(rng, 6)
    for dim, shards_of in pieces:
        heights = jnp.exp(jax.random.uniform(jax.random.fold_in(own, dim), (shards_of,), jnp.float32, low / len(pieces), high / len(pieces)))
        loudness = loudness * jnp.repeat(heights, shape[dim] // shards_of).reshape([-1 if axis == dim else 1 for axis in range(len(shape))])
    return loudness


def assign_block(stream_key, own, number, rows, count, top, limit, lean):
    sequence = jax.random.permutation(stream_key, count)
    heavy_load, usual = shares(count, rows * top, limit, lean, True), shares(count, rows * top, limit, lean, False)
    places = jnp.arange(count)

    def named(lengths, turn):
        used = int((lengths > 0).sum())
        fixed = max(1, used // 4)
        moved = fixed + (places - fixed + turn * (used - fixed)) % max(1, count - fixed)
        return jnp.zeros((count,), jnp.int32).at[sequence[jnp.where(places < fixed, places, moved)]].set(jnp.asarray(lengths, jnp.int32))

    lengths = jnp.where(number % 4 == 0, named(heavy_load, number // 4), named(usual, number - number // 4 - 1))
    mixed = jax.random.permutation(jax.random.fold_in(own, 3), count)
    source_of, sink = mixed[0:count // 2 * 2:2], mixed[1:count // 2 * 2:2]
    margin = jnp.minimum(lengths[source_of] - 1, limit - lengths[sink]) // 2
    margin = jnp.where((source_of == sequence[0]) | (sink == sequence[0]) | (lengths[sink] == 0), 0, jnp.maximum(margin, 0))
    moved = jax.random.randint(jax.random.fold_in(own, 4), (count // 2,), 0, 1 << 20) % (margin + 1)
    lengths = lengths.at[source_of].add(-moved).at[sink].add(moved)
    items = jnp.searchsorted(jnp.cumsum(lengths), jnp.arange(rows * top), side="right").astype(jnp.int32)
    table = items.reshape(top, rows).T
    table = table[jax.random.permutation(jax.random.fold_in(own, 1), rows)]
    turn = jax.random.randint(jax.random.fold_in(own, 2), (rows, 1), 0, top)
    return jnp.take_along_axis(table, (jnp.arange(top)[None, :] + turn) % top, axis=1)


def shares(amount, total, limit, skew, full):
    loads = [(1 << 20) // math.isqrt(grade ** skew) + 1 for grade in range(1, amount + 1)]
    largest = limit if full else min(limit, max(-(-total // amount), total * loads[0] // sum(loads)))
    least = 1 if total - largest >= amount - 1 else 0
    counts, rest = [largest] + [least] * (amount - 1), total - largest - least * (amount - 1)
    while rest > 0:
        movable = [i for i in range(1, amount) if counts[i] < largest] or [i for i in range(1, amount) if counts[i] < limit]
        pool, budget = sum([loads[i] for i in movable]), rest
        for i in movable:
            extra = min(limit - counts[i], max(1, budget * loads[i] // pool), rest)
            counts[i] = counts[i] + extra
            rest = rest - extra
    return np.array(counts)


def scatter_about(own_key, extent, deviation, bound, split=(), held_as=jnp.bfloat16):
    array = jax.random.normal(own_key, extent, jnp.float32) * deviation
    if len(split) > 0:
        array = level_of(own_key, extent, split, -0.22, 0.18) * array
    return jnp.clip(array, min=-bound, max=bound).astype(held_as)


def gaussian_with(own_key, dims, spread, reach, cuts, heavy, kind=jnp.bfloat16):
    values = spread * jax.random.normal(own_key, dims, jnp.float32)
    if cuts:
        values = values * level_of(own_key, dims, cuts, -0.22, 0.18)
    return jnp.clip(strengthened(values, jax.random.fold_in(own_key, 3), *heavy), -reach, reach).astype(kind)


def setup_inputs(seed: int = 0) -> dict:
    key_list = jax.random.split(jax.random.key(seed), 5)
    records = gaussian_with(key_list[0], (RECORDS, E), 1.0, 6.0, ((0, 8), (1, 4)), (0, 1, 8, 2.0))
    owner_keys = jax.random.split(jax.random.fold_in(key_list[1], 1), RECORDS // R_DEV)
    owner_turns = jax.random.permutation(jax.random.fold_in(key_list[1], 3), RECORDS // R_DEV)
    owner = jax.vmap(lambda own, number: assign_block(jax.random.fold_in(key_list[1], 2), own, number, R_DEV, N_DOM, 1, CAP, 2))(owner_keys, owner_turns).reshape((RECORDS, 1))
    entity_means = scatter_about(key_list[2], (ENTITIES, E), 1.0, 6.0, ((0, 8), (1, 4)))
    noise_bits = touch_ends(jax.random.randint(key_list[3], (SLOTS * N_DOM, ENT_DEV), 0, 8192), jax.random.fold_in(key_list[3], 1), 0, 8191).astype(jnp.int32)
    return dict(records=records, owner=owner, entity_means=entity_means, noise_bits=noise_bits)


def posterior(raw, bits, live, width):
    uniform = (bits.astype(jnp.float32) + 0.5) / 8192.0
    noise = -jnp.log(-jnp.log(uniform))
    logits = 3.0 * jnp.tanh(raw * (width ** -0.5)) + noise
    expd = jnp.exp(logits)
    return (expd / jnp.sum(expd, axis=1, keepdims=True) * live[:, None]).astype(jnp.bfloat16)


def reference(records, owner, entity_means, noise_bits):
    dest = owner[:, 0].astype(jnp.int32)
    source = (jnp.arange(RECORDS, dtype=jnp.int32) // R_DEV).astype(jnp.int32)
    onehot = (dest[:, None] == jnp.arange(N_DOM, dtype=jnp.int32)[None, :]).astype(jnp.int32)
    onehot = onehot.reshape(N_DOM, R_DEV, N_DOM)
    running = jnp.cumsum(onehot, axis=1)
    rank = (jnp.sum(running * onehot, axis=2) - 1).reshape(RECORDS).astype(jnp.int32)
    slot = (source * CAP + rank).astype(jnp.int32)

    def per_owner(gram_total, part):
        position = jnp.where(dest == part, slot, SLOTS).astype(jnp.int32)
        buffer = jnp.zeros((SLOTS + 1, E), jnp.bfloat16).at[position].set(records)[:SLOTS]
        live = jnp.zeros((SLOTS + 1,), jnp.float32).at[position].set(1.0)[:SLOTS]
        means = lax.dynamic_slice(entity_means, ((part * ENT_DEV).astype(jnp.int32), jnp.int32(0)), (ENT_DEV, E))
        bits = lax.dynamic_slice(noise_bits, ((part * SLOTS).astype(jnp.int32), jnp.int32(0)), (SLOTS, ENT_DEV))
        raw = jnp.dot(buffer, means.T, preferred_element_type=jnp.float32)
        weights = posterior(raw, bits, live, E)
        sums = jnp.dot(weights.T, buffer, preferred_element_type=jnp.float32)
        mass = jnp.sum(weights.astype(jnp.float32), axis=0)
        updated = (sums + 1.0 * means.astype(jnp.float32)) / (mass[:, None] + 1.0)
        recon = jnp.dot(weights, means, preferred_element_type=jnp.float32)
        residual = ((buffer.astype(jnp.float32) - recon) * live[:, None]).astype(jnp.bfloat16)
        term = jnp.dot(residual.T, residual, preferred_element_type=jnp.float32)
        return gram_total + term, updated

    gram_total, updated = lax.scan(per_owner, jnp.zeros((E, E), jnp.float32), jnp.arange(N_DOM, dtype=jnp.int32))
    return updated.reshape(ENTITIES, E), gram_total / RECORDS
```

```python
import functools

import jax
import jax.numpy as jnp
from jax import lax
from jax.experimental import pallas as pl
from jax.experimental.pallas import tpu as pltpu
from jax.sharding import PartitionSpec as P


def posterior(raw, bits, live, width):
    uniform = (bits.astype(jnp.float32) + 0.5) / 8192.0
    noise = -jnp.log(-jnp.log(uniform))
    logits = 3.0 * jnp.tanh(raw * width ** (-0.5)) + noise
    expd = jnp.exp(logits)
    return (expd / jnp.sum(expd, axis=1, keepdims=True) * live[:, None]).astype(jnp.bfloat16)


def shards(records, owner, entity_means, noise_bits):
    dom_count = lax.axis_size("dom")
    attr_count = lax.axis_size("attr")
    rec_dev, feat_cols = records.shape
    slot_count = 2 * rec_dev
    capacity = slot_count // dom_count
    width = feat_cols * attr_count
    total_records = rec_dev * dom_count
    dest = owner[:, 0]
    onehot = (dest[:, None] == jnp.arange(dom_count, dtype=jnp.int32)[None, :]).astype(jnp.float32)
    order = jnp.arange(rec_dev, dtype=jnp.int32)
    earlier = (order[:, None] >= order[None, :]).astype(jnp.bfloat16)
    running = jnp.dot(earlier, onehot.astype(jnp.bfloat16), preferred_element_type=jnp.float32)
    rank = jnp.sum(running * onehot, axis=1).astype(jnp.int32) - 1
    position = dest * capacity + rank
    packed = jnp.zeros((slot_count, feat_cols), jnp.bfloat16).at[position].set(records)
    flag_buf = (
        jnp.zeros((slot_count,), jnp.bfloat16).at[position].set(jnp.ones((rec_dev,), jnp.bfloat16))
    )
    arrived, arrived_flags = (
        lax.all_to_all(
            packed.reshape(dom_count, capacity, feat_cols),
            "dom",
            split_axis=0,
            concat_axis=0,
            tiled=True,
        ),
        lax.all_to_all(
            flag_buf.reshape(dom_count, capacity), "dom", split_axis=0, concat_axis=0, tiled=True
        ),
    )
    arrived = arrived.reshape(slot_count, feat_cols)
    live = arrived_flags.reshape(slot_count).astype(jnp.float32)
    raw = lax.psum(jnp.dot(arrived, entity_means.T, preferred_element_type=jnp.float32), "attr")
    weights = posterior(raw, noise_bits, live, width)
    sums_cols = jnp.dot(weights.T, arrived, preferred_element_type=jnp.float32)
    mass_col = jnp.sum(weights.astype(jnp.float32), axis=0)[:, None]
    recon = jnp.dot(weights, entity_means, preferred_element_type=jnp.float32)
    col_resid = ((arrived.astype(jnp.float32) - recon) * live[:, None]).astype(jnp.bfloat16)
    residual = lax.all_to_all(col_resid, "attr", split_axis=0, concat_axis=1, tiled=True)
    new_means = (sums_cols + 1.0 * entity_means.astype(jnp.float32)) / (mass_col + 1.0)
    term = lax.dot_general(
        residual, residual, (((0,), (0,)), ((), ())), preferred_element_type=jnp.float32
    )
    gram = lax.psum_scatter(term / total_records, ("dom", "attr"), scatter_dimension=0, tiled=True)
    return (new_means, gram)

MESH = pl.DeviceIdType.MESH
F32, BF16 = jnp.float32, jnp.bfloat16
GROUP = 2
CHUNKS = 4


def nt(a, b):
    return lax.dot_general(a, b, (((1,), (1,)), ((), ())), preferred_element_type=F32)


def nn(a, b):
    return jnp.dot(a, b, preferred_element_type=F32)


def remote(src, dst, send_sem, recv_sem, dev):
    return pltpu.make_async_remote_copy(
        src_ref=src, dst_ref=dst, send_sem=send_sem, recv_sem=recv_sem, device_id=dev, device_id_type=MESH
    )


def sweep_kernel(
    n, na, owner_ref, records_ref, means_ref, noise_ref, new_ref, gram_ref,
    rank_ref, meta_ref, metas, packed, x_ref, m_ref, bits_ref, w_ref, wt_ref, r_ref, rt_ref,
    mass_ref, masses, s_send, s_keep, s_recv, s_send2, s_recv2,
    g_send, g_keep, g_recv, gx_send, gx_recv, gy_send, gy_recv, gz_send, gz_recv,
    rec_send, rec_recv, meta_send, meta_recv, mean_send, mean_recv, bits_sem,
    mass_send, mass_recv, sum_send, sum_recv, gc_ssem, gc_rsem, gx_ssem, gx_rsem, gy_ssem, gy_rsem,
    gz_ssem, gz_rsem, ys_ssem, ys_rsem,
):
    rec_dev, feats = records_ref.shape
    ents = means_ref.shape[0]
    cap = 2 * rec_dev // n
    sub = cap // na
    width = feats * na
    d, q = lax.axis_index("dom"), lax.axis_index("attr")
    me = d * na + q
    total = n * na
    x_bit, z = lax.rem(d, 2), d // 2
    c_bit, y_bit = lax.rem(q, 2), q // 2
    nz = n // 2

    barrier = pltpu.get_barrier_semaphore()

    @pl.loop(1, total)
    def _(i):
        dev = lax.rem(me + i, total)
        pl.semaphore_signal(barrier, inc=1, device_id=(dev // na, lax.rem(dev, na)), device_id_type=MESH)

    def bits_copy(s):
        rows = pl.ds(pl.multiple_of(s * cap + q * sub, sub), sub)
        return pltpu.make_async_copy(
            noise_ref.at[rows, :], bits_ref.at[pl.ds(pl.multiple_of(s * sub, sub), sub), :], bits_sem.at[s]
        )

    @pl.loop(0, n)
    def _(s):
        bits_copy(s).start()

    blk = 256
    ids = lax.broadcasted_iota(jnp.int32, (n, blk), 0)
    upper = (
        lax.broadcasted_iota(jnp.int32, (blk, blk), 0) <= lax.broadcasted_iota(jnp.int32, (blk, blk), 1)
    ).astype(F32).astype(BF16)
    carry = jnp.zeros((n, 1), F32)
    for b in range(rec_dev // blk):
        cols = slice(b * blk, (b + 1) * blk)
        hot = (ids == owner_ref[:, cols]).astype(F32)
        run = nn(hot.astype(BF16), upper) + carry
        rank_ref[:, cols] = (jnp.sum(run * hot, axis=0, keepdims=True) - 1.0).astype(jnp.int32)
        carry = carry + jnp.sum(hot, axis=1, keepdims=True)
    counts = jnp.broadcast_to(carry, (n, 128)).astype(jnp.int32)
    meta_ref[...] = counts
    metas[d] = counts
    m_ref[q] = means_ref[...]

    def plane(i):
        far, across, near = lax.rem(z + 2, nz), nz - 1 - z, z + 1 - 2 * lax.rem(z, 2)
        return jnp.where(i == 0, far, jnp.where(i == 1, across, jnp.where(i == 2, z, near)))

    def target(t):
        return plane(t // 2) * 2 + lax.rem(x_bit + t, 2)

    def source_plane(p):
        return plane(lax.rem(p + 2, nz))

    def mean_copy(j, peer):
        return remote(means_ref, m_ref.at[q], mean_send.at[j], mean_recv.at[q], (d, peer))

    def meta_copy(t, o):
        return remote(meta_ref, metas.at[d], meta_send.at[t], meta_recv.at[d], (o, q))

    def rec_copy(t, j, o):
        return remote(
            packed.at[t, pl.ds(j * sub, sub), :],
            x_ref.at[q, pl.ds(pl.multiple_of(d * sub, sub), sub), :],
            rec_send.at[t, j], rec_recv.at[d, q], (o, j),
        )

    def pack(t):
        pos = jnp.where(owner_ref[...] == target(t), rank_ref[...], -1)
        hot = (lax.broadcasted_iota(jnp.int32, (cap, rec_dev), 0) == pos).astype(F32).astype(BF16)
        packed[t] = nn(hot, records_ref[...]).astype(BF16)

    def dispatch(t):
        o = target(t)
        for j in range(na):
            mine = jnp.logical_and(o == d, q == j)

            @pl.when(jnp.logical_not(mine))
            def _():
                rec_copy(t, j, o).start()

            @pl.when(mine)
            def _():
                x_ref[j, pl.ds(pl.multiple_of(d * sub, sub), sub), :] = packed[t, pl.ds(j * sub, sub), :]

        @pl.when(o != d)
        def _():
            meta_copy(t, o).start()

    pack(0)
    pl.semaphore_wait(barrier, total - 1)
    for j in range(1, na):
        mean_copy(j, lax.rem(q + j, na)).start()
    dispatch(0)

    @pl.loop(1, n)
    def _(t):
        pack(t)
        dispatch(t)

    rows = GROUP * sub
    out_rows = width // total
    quarter = nz * out_rows
    part = width // CHUNKS
    order = ((1, 1), (1, 0), (0, 1), (0, 0))
    core_peer, y_peer = q + 1 - 2 * c_bit, lax.rem(q + 2, na)
    x_peer = d + 1 - 2 * x_bit

    mass_ref[...] = jnp.zeros_like(mass_ref)
    s_send[...] = jnp.zeros_like(s_send)
    s_keep[...] = jnp.zeros_like(s_keep)
    g_send[...] = jnp.zeros_like(g_send)
    g_keep[...] = jnp.zeros_like(g_keep)

    for j in range(1, na):
        src = lax.rem(q + j, na)
        remote(means_ref, m_ref.at[src], mean_send.at[j], mean_recv.at[src], (d, src)).wait_recv()

    def score(p):
        zs = source_plane(p)
        for t in range(GROUP):
            s = zs * GROUP + t

            @pl.when(s != d)
            def _():
                remote(meta_ref, metas.at[s], meta_send.at[0], meta_recv.at[s], (d, q)).wait_recv()

            bits_copy(s).wait()
            for a in range(na):
                @pl.when(jnp.logical_not(jnp.logical_and(s == d, q == a)))
                def _():
                    remote(
                        packed.at[0, pl.ds(0, sub), :],
                        x_ref.at[a, pl.ds(pl.multiple_of(s * sub, sub), sub), :],
                        rec_send.at[0, a], rec_recv.at[s, a], (d, a),
                    ).wait_recv()

        at = pl.ds(pl.multiple_of(zs * rows, rows), rows)
        raw = nt(x_ref[0, at, :], m_ref[0])
        for a in range(1, na):
            raw = raw + nt(x_ref[a, at, :], m_ref[a])
        uniform = (bits_ref[at, :].astype(F32) + 0.5) / 8192.0
        expd = jnp.exp(3.0 * jnp.tanh(raw * width ** (-0.5))) / (-jnp.log(uniform))
        row = lax.broadcasted_iota(jnp.int32, (rows, 1), 0)
        live = jnp.zeros((rows, 1), F32)
        for t in range(GROUP):
            cnt = metas[zs * GROUP + t, pl.ds(d, 1), :][:, :1]
            inside = jnp.logical_and(row >= t * sub, row < (t + 1) * sub)
            live = live + jnp.where(jnp.logical_and(inside, row - t * sub + q * sub < cnt), 1.0, 0.0)
        w = (expd * (live / jnp.sum(expd, axis=1, keepdims=True))).astype(BF16)
        w_ref[...] = w
        mass_ref[...] += jnp.broadcast_to(jnp.sum(w.astype(F32), axis=0, keepdims=True), mass_ref.shape)
        for a in range(na):
            recon = nn(w, m_ref[a])
            res = (x_ref[a, at, :].astype(F32) - recon) * live
            r_ref[:, a * feats:(a + 1) * feats] = res.astype(BF16)
        for b in range(width // 128):
            cols = slice(b * 128, (b + 1) * 128)
            rt_ref[pl.ds(b * 128 // out_rows, 128 // out_rows)] = (
                r_ref[:, cols].T.reshape(128 // out_rows, out_rows, rows)
            )
        for b in range(ents // 128):
            cols = slice(b * 128, (b + 1) * 128)
            wt_ref[cols, :] = w_ref[:, cols].T

    def partial_sums(p, t, core):
        at = pl.ds(pl.multiple_of(source_plane(p) * rows, rows), rows)
        return nn(wt_ref[...], x_ref[(y_bit if t == 0 else 1 - y_bit) * 2 + core, at, :])

    def gram_rows(dx, dy, core, c):
        xb = x_bit if dx == 0 else 1 - x_bit
        yb = y_bit if dy == 0 else 1 - y_bit
        lhs = jnp.concatenate([rt_ref[(zz * 2 + xb) * na + yb * 2 + core] for zz in range(nz)], axis=0)
        return nn(lhs, r_ref[:, c * part:(c + 1) * part])

    def add_gram(out_ref, core, c):
        for i, (dx, dy) in enumerate(order):
            out_ref[c, i * quarter:(i + 1) * quarter, :] += gram_rows(dx, dy, core, c)

    @pl.loop(0, nz - 1)
    def _(p):
        score(p)
        for t in range(2):
            s_send[t] += partial_sums(p, t, 1 - c_bit)
            s_keep[t] += partial_sums(p, t, c_bit)
        for c in range(CHUNKS):
            add_gram(g_send, 1 - c_bit, c)
            add_gram(g_keep, c_bit, c)

    def mass_copy(j, peer):
        return remote(mass_ref, masses.at[q], mass_send.at[j], mass_recv.at[q], (d, peer))

    def core_sums(t):
        return remote(s_send.at[t], s_recv.at[t], sum_send.at[t], sum_recv.at[t], (d, core_peer))

    def y_sums():
        return remote(s_send2, s_recv2, ys_ssem.at[0], ys_rsem.at[0], (d, y_peer))

    def core_gram(c):
        return remote(g_send.at[c], g_recv.at[c], gc_ssem.at[c], gc_rsem.at[c], (d, core_peer))

    def x_gram(c):
        return remote(gx_send.at[c], gx_recv.at[c], gx_ssem.at[c], gx_rsem.at[c], (x_peer, q))

    def y_gram(c):
        return remote(gy_send.at[c], gy_recv.at[c], gy_ssem.at[c], gy_rsem.at[c], (d, y_peer))

    def z_copy(c, j):
        to = lax.rem(z + j, nz)
        return remote(
            gz_send.at[c, pl.ds(pl.multiple_of(to * out_rows, out_rows), out_rows), :],
            gz_recv.at[c, j - 1], gz_ssem.at[c, j - 1], gz_rsem.at[c, j - 1], (to * 2 + x_bit, q),
        )

    top, low = slice(0, 2 * quarter), slice(2 * quarter, 4 * quarter)
    third, last = slice(2 * quarter, 3 * quarter), slice(3 * quarter, 4 * quarter)

    def to_x(c):
        core_gram(c).wait_recv()
        gx_send[c] = (g_keep[c, top, :] + g_recv[c, top, :]).astype(BF16)
        x_gram(c).start()
        g_keep[c, low, :] += g_recv[c, low, :]

    def to_y(c):
        x_gram(c).wait_recv()
        gy_send[c] = (g_keep[c, third, :] + gx_recv[c, :quarter, :].astype(F32)).astype(BF16)
        y_gram(c).start()
        g_keep[c, last, :] += gx_recv[c, quarter:, :].astype(F32)

    def to_z(c):
        y_gram(c).wait_recv()
        full = g_keep[c, last, :] + gy_recv[c].astype(F32)
        gz_send[c] = full.astype(BF16)
        for j in range(1, nz):
            z_copy(c, j).start()
        g_keep[c, last, :] = full

    final = nz - 1
    score(final)
    add_gram(g_send, 1 - c_bit, 0)
    core_gram(0).start()
    s_send[1] += partial_sums(final, 1, 1 - c_bit)
    core_sums(1).start()
    add_gram(g_keep, c_bit, 0)
    add_gram(g_send, 1 - c_bit, 1)
    core_gram(1).start()
    to_x(0)
    s_keep[1] += partial_sums(final, 1, c_bit)
    core_sums(1).wait_recv()
    s_send2[...] = (s_keep[1] + s_recv[1]).astype(BF16)
    y_sums().start()
    masses[q] = mass_ref[...]
    for j in range(1, na):
        mass_copy(j, lax.rem(q + j, na)).start()
    add_gram(g_keep, c_bit, 1)
    to_x(1)
    for c in range(2, CHUNKS):
        add_gram(g_send, 1 - c_bit, c)
        core_gram(c).start()
        add_gram(g_keep, c_bit, c)
        to_x(c)
    s_send[0] += partial_sums(final, 0, 1 - c_bit)
    core_sums(0).start()
    s_keep[0] += partial_sums(final, 0, c_bit)
    for c in range(CHUNKS - 1):
        to_y(c)
        if c > 0:
            to_z(c - 1)
    core_sums(0).wait_recv()
    for j in range(1, na):
        src = lax.rem(q + j, na)
        remote(mass_ref, masses.at[src], mass_send.at[j], mass_recv.at[src], (d, src)).wait_recv()
    y_sums().wait_recv()
    mass = masses[0]
    for a in range(1, na):
        mass = mass + masses[a]
    col = jnp.broadcast_to(mass[:1, :], (128, ents)).T
    for b in range(feats // 128):
        cols = slice(b * 128, (b + 1) * 128)
        full = s_keep[0, :, cols] + s_recv[0, :, cols] + s_recv2[:, cols].astype(F32)
        new_ref[:, cols] = (full + 1.0 * means_ref[:, cols].astype(F32)) / (col + 1.0)
    to_y(CHUNKS - 1)
    to_z(CHUNKS - 2)
    to_z(CHUNKS - 1)
    for c in range(CHUNKS):
        acc = g_keep[c, pl.ds(pl.multiple_of(3 * quarter + z * out_rows, out_rows), out_rows), :]
        for j in range(1, nz):
            z_copy(c, j).wait_recv()
            acc = acc + gz_recv[c, j - 1].astype(F32)
        gram_ref[:, c * part:(c + 1) * part] = acc

    for j in range(1, na):
        mean_copy(j, lax.rem(q + j, na)).wait_send()
        mass_copy(j, lax.rem(q + j, na)).wait_send()
    for t in range(2):
        core_sums(t).wait_send()
    y_sums().wait_send()
    for c in range(CHUNKS):
        core_gram(c).wait_send()
        x_gram(c).wait_send()
        y_gram(c).wait_send()
        for j in range(1, nz):
            z_copy(c, j).wait_send()

    @pl.loop(0, n)
    def _(t):
        o = target(t)

        @pl.when(o != d)
        def _():
            meta_copy(t, o).wait_send()

        for j in range(na):
            @pl.when(jnp.logical_not(jnp.logical_and(o == d, q == j)))
            def _():
                rec_copy(t, j, o).wait_send()


def finish_kernel(records, means_ref, gram_ref, means_out, gram_out):
    means_out[...] = means_ref[...]
    gram_out[...] = gram_ref[...] / records


def fused(n, na, records, owner, entity_means, noise_bits):
    rec_dev, feats = records.shape
    ents = entity_means.shape[0]
    cap = 2 * rec_dev // n
    slots = 2 * rec_dev // na
    rows = GROUP * (cap // na)
    width = feats * na
    out_rows = width // (n * na)
    nz = n // 2
    quarter = nz * out_rows
    part = width // CHUNKS
    vm, dma = pltpu.VMEM, pltpu.SemaphoreType.DMA
    vspec = pl.BlockSpec(memory_space=pltpu.VMEM)
    scratch = [
        vm((1, rec_dev), jnp.int32), vm((n, 128), jnp.int32), vm((n, n, 128), jnp.int32),
        vm((n, cap, feats), BF16), vm((na, slots, feats), BF16), vm((na, ents, feats), BF16),
        vm((slots, ents), jnp.int32), vm((rows, ents), BF16), vm((ents, rows), BF16),
        vm((rows, width), BF16), vm((n * na, out_rows, rows), BF16),
        vm((8, ents), F32), vm((na, 8, ents), F32),
        vm((2, ents, feats), F32), vm((2, ents, feats), F32), vm((2, ents, feats), F32),
        vm((ents, feats), BF16), vm((ents, feats), BF16),
        vm((CHUNKS, 4 * quarter, part), F32), vm((CHUNKS, 4 * quarter, part), F32),
        vm((CHUNKS, 4 * quarter, part), F32),
        vm((CHUNKS, 2 * quarter, part), BF16), vm((CHUNKS, 2 * quarter, part), BF16),
        vm((CHUNKS, quarter, part), BF16), vm((CHUNKS, quarter, part), BF16),
        vm((CHUNKS, quarter, part), BF16), vm((CHUNKS, nz - 1, out_rows, part), BF16),
        dma((n, na)), dma((n, na)), dma((n,)), dma((n,)), dma((na,)), dma((na,)), dma((n,)),
        dma((na,)), dma((na,)), dma((2,)), dma((2,)),
        *(dma((CHUNKS,)) for _ in range(6)), dma((CHUNKS, nz - 1)), dma((CHUNKS, nz - 1)),
        dma((1,)), dma((1,)),
    ]
    new_means, gram = pl.pallas_call(
        functools.partial(sweep_kernel, n, na),
        out_shape=(jax.ShapeDtypeStruct((ents, feats), F32), jax.ShapeDtypeStruct((out_rows, width), F32)),
        in_specs=[vspec, vspec, vspec, pl.BlockSpec(memory_space=pl.ANY)],
        out_specs=(vspec, vspec),
        scratch_shapes=scratch,
        compiler_params=pltpu.CompilerParams(
            collective_id=0, has_side_effects=True, vmem_limit_bytes=56 * 1024 * 1024
        ),
    )(owner.reshape(1, rec_dev), records, entity_means, noise_bits)
    return pl.pallas_call(
        functools.partial(finish_kernel, float(rec_dev * n)),
        out_shape=(jax.ShapeDtypeStruct((ents, feats), F32), jax.ShapeDtypeStruct((out_rows, width), F32)),
        in_specs=[vspec, vspec],
        out_specs=(vspec, vspec),
    )(new_means, gram)


def sweep(records, owner, entity_means, noise_bits):
    n, na = lax.axis_size("dom"), lax.axis_size("attr")
    rec_dev, feats = records.shape
    sub = 2 * rec_dev // n // na
    out_rows = feats // n
    if na == 4 and n == 8 and sub % 16 == 0 and out_rows % 16 == 0:
        return fused(n, na, records, owner, entity_means, noise_bits)
    return shards(records, owner, entity_means, noise_bits)


def solution(mesh):
    in_specs = (P("dom", "attr"), P("dom", None), P("dom", "attr"), P("dom", None))
    out_specs = (P("dom", "attr"), P(("dom", "attr"), None))
    return jax.shard_map(sweep, mesh=mesh, in_specs=in_specs, out_specs=out_specs, check_vma=False)
```

```python
import functools

import jax
import jax.numpy as jnp
from jax import lax
from jax.experimental import pallas as pl
from jax.experimental.pallas import tpu as pltpu
from jax.sharding import PartitionSpec as P


def posterior(raw, bits, live, width):
    uniform = (bits.astype(jnp.float32) + 0.5) / 8192.0
    noise = -jnp.log(-jnp.log(uniform))
    logits = 3.0 * jnp.tanh(raw * width ** (-0.5)) + noise
    expd = jnp.exp(logits)
    return (expd / jnp.sum(expd, axis=1, keepdims=True) * live[:, None]).astype(jnp.bfloat16)


def shards(records, owner, entity_means, noise_bits):
    dom_count = lax.axis_size("dom")
    attr_count = lax.axis_size("attr")
    rec_dev, feat_cols = records.shape
    slot_count = 2 * rec_dev
    capacity = slot_count // dom_count
    width = feat_cols * attr_count
    total_records = rec_dev * dom_count
    dest = owner[:, 0]
    onehot = (dest[:, None] == jnp.arange(dom_count, dtype=jnp.int32)[None, :]).astype(jnp.float32)
    order = jnp.arange(rec_dev, dtype=jnp.int32)
    earlier = (order[:, None] >= order[None, :]).astype(jnp.bfloat16)
    running = jnp.dot(earlier, onehot.astype(jnp.bfloat16), preferred_element_type=jnp.float32)
    rank = jnp.sum(running * onehot, axis=1).astype(jnp.int32) - 1
    position = dest * capacity + rank
    packed = jnp.zeros((slot_count, feat_cols), jnp.bfloat16).at[position].set(records)
    flag_buf = (
        jnp.zeros((slot_count,), jnp.bfloat16).at[position].set(jnp.ones((rec_dev,), jnp.bfloat16))
    )
    arrived, arrived_flags = (
        lax.all_to_all(
            packed.reshape(dom_count, capacity, feat_cols),
            "dom",
            split_axis=0,
            concat_axis=0,
            tiled=True,
        ),
        lax.all_to_all(
            flag_buf.reshape(dom_count, capacity), "dom", split_axis=0, concat_axis=0, tiled=True
        ),
    )
    arrived = arrived.reshape(slot_count, feat_cols)
    live = arrived_flags.reshape(slot_count).astype(jnp.float32)
    raw = lax.psum(jnp.dot(arrived, entity_means.T, preferred_element_type=jnp.float32), "attr")
    weights = posterior(raw, noise_bits, live, width)
    sums_cols = jnp.dot(weights.T, arrived, preferred_element_type=jnp.float32)
    mass_col = jnp.sum(weights.astype(jnp.float32), axis=0)[:, None]
    recon = jnp.dot(weights, entity_means, preferred_element_type=jnp.float32)
    col_resid = ((arrived.astype(jnp.float32) - recon) * live[:, None]).astype(jnp.bfloat16)
    residual = lax.all_to_all(col_resid, "attr", split_axis=0, concat_axis=1, tiled=True)
    new_means = (sums_cols + 1.0 * entity_means.astype(jnp.float32)) / (mass_col + 1.0)
    term = lax.dot_general(
        residual, residual, (((0,), (0,)), ((), ())), preferred_element_type=jnp.float32
    )
    gram = lax.psum_scatter(term / total_records, ("dom", "attr"), scatter_dimension=0, tiled=True)
    return (new_means, gram)

MESH = pl.DeviceIdType.MESH
F32, BF16 = jnp.float32, jnp.bfloat16
GROUP = 2
LANES = 128
TILES = 5
MIRROR = 3


def nt(a, b):
    return lax.dot_general(a, b, (((1,), (1,)), ((), ())), preferred_element_type=F32)


def nn(a, b):
    return jnp.dot(a, b, preferred_element_type=F32)


def remote(src, dst, send_sem, recv_sem, dev):
    return pltpu.make_async_remote_copy(
        src_ref=src, dst_ref=dst, send_sem=send_sem, recv_sem=recv_sem, device_id=dev, device_id_type=MESH
    )


def landed(ref, sem):
    pltpu.make_async_copy(ref, ref, sem).wait()


def sweep_kernel(
    n, na, owner_hbm, records_hbm, means_hbm, noise_ref, new_hbm, gram_hbm,
    owner_ref, records_ref, new_ref, gram_ref,
    rank_ref, meta_ref, metas, packed, x_ref, m_ref, bits_ref, gumbel_ref, live_ref, w_ref, wt_ref, r_ref, rt_ref,
    mass_ref, masses, diag_ref, diag_send, diags, s_send, s_keep, s_recv, s_send2, s_recv2,
    g_acc, g_send, g_recv, gx_send, gx_recv, gy_send, gy_recv, gz_keep, gz_send, gz_recv, gm_send, gm_recv, p_ref,
    in_sem, out_sem, rec_send, rec_recv, meta_send, meta_recv, mean_send, mean_recv, bits_sem,
    mass_ssem, mass_rsem, diag_ssem, diag_rsem, sum_ssem, sum_rsem, gc_ssem, gc_rsem, gx_ssem, gx_rsem, gy_ssem, gy_rsem,
    gz_ssem, gz_rsem, gm_ssem, gm_rsem, ys_ssem, ys_rsem,
):
    rec_dev, feats = records_ref.shape
    ents = m_ref.shape[1]
    cap = 2 * rec_dev // n
    sub = cap // na
    width = feats * na
    d, q = lax.axis_index("dom"), lax.axis_index("attr")
    me = d * na + q
    total = n * na
    x_bit, z = lax.rem(d, 2), d // 2
    c_bit, y_bit = lax.rem(q, 2), q // 2
    nz = n // 2
    rows = GROUP * sub
    out_rows = width // total

    barrier = pltpu.get_barrier_semaphore()

    @pl.loop(1, total)
    def _(i):
        dev = lax.rem(me + i, total)
        pl.semaphore_signal(barrier, inc=1, device_id=(dev // na, lax.rem(dev, na)), device_id_type=MESH)

    owner_in = pltpu.make_async_copy(owner_hbm, owner_ref, in_sem.at[0])
    records_in = pltpu.make_async_copy(records_hbm, records_ref, in_sem.at[1])
    means_in = pltpu.make_async_copy(means_hbm, m_ref.at[q], in_sem.at[2])
    owner_in.start()
    records_in.start()
    means_in.start()

    def bits_copy(s):
        at = pl.ds(pl.multiple_of(s * cap + q * sub, sub), sub)
        return pltpu.make_async_copy(
            noise_ref.at[at, :], bits_ref.at[pl.ds(pl.multiple_of(s * sub, sub), sub), :], bits_sem.at[0]
        )

    @pl.loop(0, n)
    def _(s):
        bits_copy(s).start()

    owner_in.wait()
    blk = 256
    ids = lax.broadcasted_iota(jnp.int32, (n, blk), 0)
    upper = (
        lax.broadcasted_iota(jnp.int32, (blk, blk), 0) <= lax.broadcasted_iota(jnp.int32, (blk, blk), 1)
    ).astype(F32).astype(BF16)
    cuts = [slice(b * blk, (b + 1) * blk) for b in range(rec_dev // blk)]
    hots = [(ids == owner_ref[:, cols]).astype(F32) for cols in cuts]
    runs = nn(jnp.concatenate(hots, axis=0).astype(BF16), upper)
    carry = jnp.zeros((n, 1), F32)
    for b, cols in enumerate(cuts):
        run = runs[b * n:(b + 1) * n, :] + carry
        rank_ref[:, cols] = (jnp.sum(run * hots[b], axis=0, keepdims=True) - 1.0).astype(jnp.int32)
        carry = carry + jnp.sum(hots[b], axis=1, keepdims=True)
    counts = jnp.broadcast_to(carry, (n, LANES)).astype(jnp.int32)
    meta_ref[...] = counts
    metas[d] = counts

    def plane(i):
        far, across, near = lax.rem(z + 2, nz), nz - 1 - z, z + 1 - 2 * lax.rem(z, 2)
        return jnp.where(i == 0, far, jnp.where(i == 1, across, jnp.where(i == 2, z, near)))

    def target(t):
        return plane(t // 2) * 2 + lax.rem(x_bit + t, 2)

    def source_plane(p):
        return plane(lax.rem(p + 2, nz))

    def mean_copy(peer):
        return remote(m_ref.at[q], m_ref.at[q], mean_send.at[0], mean_recv.at[0], (d, peer))

    def meta_copy(o):
        return remote(meta_ref, metas.at[d], meta_send.at[0], meta_recv.at[z], (o, q))

    def rec_copy(t, j, o):
        return remote(
            packed.at[pl.ds(pl.multiple_of(t * cap + j * sub, sub), sub), :],
            x_ref.at[q, pl.ds(pl.multiple_of(d * sub, sub), sub), :],
            rec_send.at[0], rec_recv.at[z], (o, j),
        )

    def pack(t):
        pos = jnp.where(owner_ref[...] == target(t), rank_ref[...], -1)
        hot = (lax.broadcasted_iota(jnp.int32, (cap, rec_dev), 0) == pos).astype(F32).astype(BF16)
        packed[pl.ds(pl.multiple_of(t * cap, cap), cap), :] = nn(hot, records_ref[...]).astype(BF16)

    def dispatch(t):
        o = target(t)
        for j in range(na):
            mine = jnp.logical_and(o == d, q == j)

            @pl.when(jnp.logical_not(mine))
            def _():
                rec_copy(t, j, o).start()

            @pl.when(mine)
            def _():
                x_ref[j, pl.ds(pl.multiple_of(d * sub, sub), sub), :] = (
                    packed[pl.ds(pl.multiple_of(t * cap + j * sub, sub), sub), :]
                )

        @pl.when(o != d)
        def _():
            meta_copy(o).start()

    records_in.wait()
    pack(0)
    means_in.wait()
    pl.semaphore_wait(barrier, total - 1)
    dispatch(0)
    for j in range(1, na):
        mean_copy(lax.rem(q + j, na)).start()

    @pl.loop(1, n)
    def _(t):
        pack(t)
        dispatch(t)

    core_peer, y_peer = q + 1 - 2 * c_bit, lax.rem(q + 2, na)
    x_peer = d + 1 - 2 * x_bit
    order = [(dc, dx, dy) for dc in (1, 0) for dx in (1, 0) for dy in (1, 0)]
    mine = c_bit * 4 + x_bit * 2 + y_bit

    def flip(bit, by):
        return 1 - bit if by else bit

    mass_ref[...] = jnp.zeros_like(mass_ref)
    diag_ref[...] = jnp.zeros_like(diag_ref)
    s_send[...] = jnp.zeros_like(s_send)
    s_keep[...] = jnp.zeros_like(s_keep)
    g_acc[...] = jnp.zeros_like(g_acc)

    landed(m_ref.at[pl.ds(0, na - 1)], mean_recv.at[0])
    landed(bits_ref, bits_sem.at[0])

    @pl.loop(0, n)
    def _(s):
        at = pl.ds(pl.multiple_of(s * sub, sub), sub)
        gumbel_ref[at, :] = 1.0 / (-jnp.log((bits_ref[at, :].astype(F32) + 0.5) / 8192.0))

    def weigh(p):
        zs = source_plane(p)

        @pl.when(zs == z)
        def _():
            landed(metas.at[pl.ds(0, GROUP - 1)], meta_recv.at[zs])
            landed(packed.at[pl.ds(0, (GROUP * na - 1) * sub), :], rec_recv.at[zs])

        @pl.when(zs != z)
        def _():
            landed(metas.at[pl.ds(0, GROUP)], meta_recv.at[zs])
            landed(packed.at[pl.ds(0, GROUP * na * sub), :], rec_recv.at[zs])

        at = pl.ds(pl.multiple_of(zs * rows, rows), rows)
        raw = nt(x_ref[0, at, :], m_ref[0])
        for a in range(1, na):
            raw = raw + nt(x_ref[a, at, :], m_ref[a])
        expd = jnp.exp(3.0 * jnp.tanh(raw * width ** (-0.5))) * gumbel_ref[at, :]
        row = lax.broadcasted_iota(jnp.int32, (rows, 1), 0)
        live = jnp.zeros((rows, 1), F32)
        for t in range(GROUP):
            cnt = metas[zs * GROUP + t, pl.ds(d, 1), :][:, :1]
            inside = jnp.logical_and(row >= t * sub, row < (t + 1) * sub)
            live = live + jnp.where(jnp.logical_and(inside, row - t * sub + q * sub < cnt), 1.0, 0.0)
        w = (expd * (live / jnp.sum(expd, axis=1, keepdims=True))).astype(BF16)
        w_ref[...] = w
        live_ref[...] = jnp.broadcast_to(live, live_ref.shape)
        mass_ref[...] += jnp.broadcast_to(jnp.sum(w.astype(F32), axis=0, keepdims=True), mass_ref.shape)
        for b in range(ents // LANES):
            cols = slice(b * LANES, (b + 1) * LANES)
            wt_ref[cols, :] = w_ref[:, cols].T

    def residual(p):
        at = pl.ds(pl.multiple_of(source_plane(p) * rows, rows), rows)
        w, live = w_ref[...], live_ref[:, :1]
        for a in range(na):
            recon = nn(w, m_ref[a])
            res = ((x_ref[a, at, :].astype(F32) - recon) * live).astype(BF16)
            r_ref[:, a * feats:(a + 1) * feats] = res
            wide = res.astype(F32)
            square = jnp.sum(wide * wide, axis=0, keepdims=True)
            diag_ref[:, a * feats:(a + 1) * feats] += jnp.broadcast_to(square, (8, feats))
        for b in range(n):
            turned = r_ref[:, b * LANES:(b + 1) * LANES].T
            zz, xx = b // 2, b % 2
            for e in range(na):
                g = (e % 2) * 4 + xx * 2 + e // 2
                piece = turned[e * out_rows:(e + 1) * out_rows, :]
                for copy in (g, g + 8):
                    if copy < 8 + TILES - 1:
                        rt_ref[pl.ds(copy * LANES + zz * out_rows, out_rows), :] = piece

    def partial_sums(p, t, core):
        at = pl.ds(pl.multiple_of(source_plane(p) * rows, rows), rows)
        return nn(wt_ref[...], x_ref[(y_bit if t == 0 else 1 - y_bit) * 2 + core, at, :])

    def band(k):
        dc, dx, dy = order[k]
        return flip(c_bit, dc) * 4 + flip(x_bit, dx) * 2 + flip(y_bit, dy)

    def gram_band(k):
        first = pl.multiple_of(band(k) * LANES, LANES)
        return nt(rt_ref[pl.ds(first, LANES), :], rt_ref[pl.ds(first, TILES * LANES), :])

    def add_gram(k):
        new = gram_band(k)
        for m in range(TILES):
            g_acc[m, k * LANES:(k + 1) * LANES, :] += new[:, m * LANES:(m + 1) * LANES]

    @pl.loop(0, nz - 1)
    def _(p):
        weigh(p)
        residual(p)
        for t in range(2):
            s_send[t] += partial_sums(p, t, 1 - c_bit)
            s_keep[t] += partial_sums(p, t, c_bit)
        for k in range(8):
            add_gram(k)

    def mass_copy(peer):
        return remote(mass_ref, masses.at[q], mass_ssem.at[0], mass_rsem.at[0], (d, peer))

    def diag_copy(j):
        dev = lax.rem(me + j, total)
        return remote(
            diag_send.at[dev // na], diags.at[j], diag_ssem.at[0], diag_rsem.at[0], (dev // na, lax.rem(dev, na))
        )

    def core_sums(t):
        return remote(s_send.at[t], s_recv.at[t], sum_ssem.at[0], sum_rsem.at[t], (d, core_peer))

    def y_sums(c):
        at = pl.ds(c * LANES, LANES)
        return remote(s_send2.at[at], s_recv2.at[at], ys_ssem.at[0], ys_rsem.at[0], (d, y_peer))

    def core_gram(m):
        return remote(g_send.at[m], g_recv.at[m], gc_ssem.at[0], gc_rsem.at[m], (d, core_peer))

    def x_gram(m):
        return remote(gx_send.at[m], gx_recv.at[m], gx_ssem.at[0], gx_rsem.at[m], (x_peer, q))

    def y_gram(m):
        return remote(gy_send.at[m], gy_recv.at[m], gy_ssem.at[0], gy_rsem.at[m], (d, y_peer))

    def z_copy(m, j):
        to = lax.rem(z + j, nz)
        return remote(
            gz_send.at[m, pl.ds(pl.multiple_of(to * out_rows, out_rows), out_rows), :],
            gz_recv.at[j - 1, m], gz_ssem.at[0], gz_rsem.at[0], (to * 2 + x_bit, q),
        )

    def mirror_copy(m, to):
        g = lax.rem(mine + m, 8)
        return remote(
            gm_send.at[m - 1, pl.ds(to * out_rows, out_rows), :],
            gm_recv.at[z, m - 1], gm_ssem.at[0], gm_rsem.at[0],
            (to * 2 + lax.rem(g // 2, 2), lax.rem(g, 2) * 2 + g // 4),
        )

    half, quart, eighth = 4 * LANES, 6 * LANES, 7 * LANES

    def to_x(m):
        core_gram(m).wait_recv()
        gx_send[m] = (g_acc[m, half:quart, :] + g_recv[m, :2 * LANES, :].astype(F32)).astype(BF16)
        x_gram(m).start()
        g_acc[m, quart:, :] += g_recv[m, 2 * LANES:, :].astype(F32)

    def to_y(m):
        x_gram(m).wait_recv()
        gy_send[m] = (g_acc[m, quart:eighth, :] + gx_recv[m, :LANES, :].astype(F32)).astype(BF16)
        y_gram(m).start()
        g_acc[m, eighth:, :] += gx_recv[m, LANES:, :].astype(F32)

    def to_z(m):
        y_gram(m).wait_recv()
        full = g_acc[m, eighth:, :] + gy_recv[m].astype(F32)
        gz_send[m] = full.astype(BF16)
        for j in range(1, nz):
            z_copy(m, j).start()
        gz_keep[m] = full
        if 1 <= m <= MIRROR:
            gm_send[m - 1] = full.T.astype(BF16)
            for to in range(nz):
                mirror_copy(m, to).start()

    final, pieces = nz - 1, ents // LANES
    turns = list(range(1, MIRROR + 1)) + [0, TILES - 1]
    weigh(final)
    s_send[1] += partial_sums(final, 1, 1 - c_bit)
    core_sums(1).start()
    residual(final)
    for k in range(4):
        new = gram_band(k)
        for m in range(TILES):
            at = slice(k * LANES, (k + 1) * LANES)
            g_send[m, at, :] = (g_acc[m, at, :] + new[:, m * LANES:(m + 1) * LANES]).astype(BF16)
    for m in turns:
        core_gram(m).start()
    add_gram(4)
    add_gram(5)
    for m in turns[:3]:
        to_x(m)
    s_keep[1] += partial_sums(final, 1, c_bit)
    core_sums(1).wait_recv()
    s_send2[...] = (s_keep[1] + s_recv[1]).astype(BF16)
    y_sums(0).start()
    y_sums(1).start()
    add_gram(6)
    add_gram(7)
    s_send[0] += partial_sums(final, 0, 1 - c_bit)
    core_sums(0).start()
    masses[q] = mass_ref[...]
    for j in range(1, na):
        mass_copy(lax.rem(q + j, na)).start()
    for b in range(n):
        diag_send[b] = diag_ref[:1, b * LANES:(b + 1) * LANES]
    diags[0] = diag_send[d]

    @pl.loop(1, total)
    def _(j):
        diag_copy(j).start()

    s_keep[0] += partial_sums(final, 0, c_bit)
    for i, m in enumerate(turns):
        to_y(m)
        if i < pieces - 2:
            y_sums(i + 2).start()
        if i + 3 < TILES:
            to_x(turns[i + 3])
        if i > 1:
            to_z(turns[i - 2])
    to_z(turns[-2])
    to_z(turns[-1])

    core_sums(0).wait_recv()
    landed(masses.at[pl.ds(0, na - 1)], mass_rsem.at[0])
    landed(s_recv2, ys_rsem.at[0])
    mass = masses[0]
    for a in range(1, na):
        mass = mass + masses[a]
    col = jnp.broadcast_to(mass[:1, :], (LANES, ents)).T
    for b in range(feats // LANES):
        cols = slice(b * LANES, (b + 1) * LANES)
        full = s_keep[0, :, cols] + s_recv[0, :, cols] + s_recv2[:, cols].astype(F32)
        new_ref[:, cols] = (full + 1.0 * m_ref[q, :, cols].astype(F32)) / (col + 1.0)
    new_out = pltpu.make_async_copy(new_ref, new_hbm, out_sem.at[0])
    new_out.start()

    landed(diags.at[pl.ds(1, total - 1)], diag_rsem.at[0])
    diag = jnp.broadcast_to(jnp.sum(diags[...], axis=0), (out_rows, LANES))
    row = lax.broadcasted_iota(jnp.int32, (out_rows, LANES), 0)
    lane = lax.broadcasted_iota(jnp.int32, (out_rows, LANES), 1)
    diag = jnp.sum(jnp.where(lane == row + q * out_rows, diag, 0.0), axis=1, keepdims=True)
    own_rows = pl.ds(pl.multiple_of(z * out_rows, out_rows), out_rows)
    landed(gz_recv, gz_rsem.at[0])
    for m in range(TILES):
        acc = gz_keep[m, own_rows, :]
        for j in range(1, nz):
            acc = acc + gz_recv[j - 1, m].astype(F32)
        if m == 0:
            acc = jnp.where(lane == row + z * out_rows, diag, acc)
        p_ref[lax.rem(mine + m, 8)] = acc
    landed(gm_recv, gm_rsem.at[0])
    for m in range(1, MIRROR + 1):
        acc = jnp.zeros((out_rows, LANES), F32)
        for zz in range(nz):
            acc = acc + gm_recv[zz, m - 1].astype(F32)
        p_ref[lax.rem(mine + 8 - m, 8)] = acc
    for b in range(n):
        zz, xx = b // 2, b % 2
        gram_ref[:, b * LANES:(b + 1) * LANES] = jnp.concatenate(
            [
                p_ref[(e % 2) * 4 + xx * 2 + e // 2, :, zz * out_rows:(zz + 1) * out_rows]
                for e in range(na)
            ],
            axis=1,
        )
    gram_out = pltpu.make_async_copy(gram_ref, gram_hbm, out_sem.at[1])
    gram_out.start()

    landed(m_ref.at[pl.ds(0, na - 1)], mean_send.at[0])
    landed(masses.at[pl.ds(0, na - 1)], mass_ssem.at[0])
    landed(s_send, sum_ssem.at[0])
    landed(s_send2, ys_ssem.at[0])
    landed(diags.at[pl.ds(1, total - 1)], diag_ssem.at[0])
    landed(g_send, gc_ssem.at[0])
    landed(gx_send, gx_ssem.at[0])
    landed(gy_send, gy_ssem.at[0])
    landed(gz_recv, gz_ssem.at[0])
    landed(gm_recv, gm_ssem.at[0])
    landed(metas.at[pl.ds(0, n - 1)], meta_send.at[0])
    landed(packed.at[pl.ds(0, (total - 1) * sub), :], rec_send.at[0])
    new_out.wait()
    gram_out.wait()


def finish_kernel(records, means_ref, gram_ref, means_out, gram_out):
    means_out[...] = means_ref[...]
    gram_out[...] = gram_ref[...] / records


def fused(n, na, records, owner, entity_means, noise_bits):
    rec_dev, feats = records.shape
    ents = entity_means.shape[0]
    cap = 2 * rec_dev // n
    slots = 2 * rec_dev // na
    rows = GROUP * (cap // na)
    width = feats * na
    total = n * na
    out_rows = width // total
    nz = n // 2
    vm, dma = pltpu.VMEM, pltpu.SemaphoreType.DMA
    vspec = pl.BlockSpec(memory_space=pltpu.VMEM)
    hspec = pl.BlockSpec(memory_space=pl.ANY)
    scratch = [
        vm((1, rec_dev), jnp.int32), vm((rec_dev, feats), BF16), vm((ents, feats), F32), vm((out_rows, width), F32),
        vm((1, rec_dev), jnp.int32), vm((n, LANES), jnp.int32), vm((n, n, LANES), jnp.int32),
        vm((n * cap, feats), BF16), vm((na, slots, feats), BF16), vm((na, ents, feats), BF16),
        vm((slots, ents), jnp.int32), vm((slots, ents), F32), vm((rows, LANES), F32), vm((rows, ents), BF16), vm((ents, rows), BF16),
        vm((rows, width), BF16), vm(((8 + TILES - 1) * LANES, rows), BF16),
        vm((8, ents), F32), vm((na, 8, ents), F32),
        vm((8, width), F32), vm((n, 1, LANES), F32), vm((total, 1, LANES), F32),
        vm((2, ents, feats), F32), vm((2, ents, feats), F32), vm((2, ents, feats), F32),
        vm((ents, feats), BF16), vm((ents, feats), BF16),
        vm((TILES, 8 * LANES, LANES), F32),
        vm((TILES, 4 * LANES, LANES), BF16), vm((TILES, 4 * LANES, LANES), BF16),
        vm((TILES, 2 * LANES, LANES), BF16), vm((TILES, 2 * LANES, LANES), BF16),
        vm((TILES, LANES, LANES), BF16), vm((TILES, LANES, LANES), BF16),
        vm((TILES, LANES, LANES), F32), vm((TILES, LANES, LANES), BF16),
        vm((nz - 1, TILES, out_rows, LANES), BF16),
        vm((MIRROR, LANES, LANES), BF16), vm((nz, MIRROR, out_rows, LANES), BF16),
        vm((8, out_rows, LANES), F32),
        dma((3,)), dma((2,)),
        dma((1,)), dma((nz,)), dma((1,)), dma((nz,)), *(dma((1,)) for _ in range(7)),
        dma((1,)), dma((2,)), *(dma((size,)) for _ in range(3) for size in (1, TILES)),
        *(dma((1,)) for _ in range(6)),
    ]
    new_means, gram = pl.pallas_call(
        functools.partial(sweep_kernel, n, na),
        out_shape=(jax.ShapeDtypeStruct((ents, feats), F32), jax.ShapeDtypeStruct((out_rows, width), F32)),
        in_specs=[hspec, hspec, hspec, hspec],
        out_specs=(hspec, hspec),
        scratch_shapes=scratch,
        compiler_params=pltpu.CompilerParams(
            collective_id=0, has_side_effects=True, vmem_limit_bytes=56 * 1024 * 1024
        ),
    )(owner.reshape(1, rec_dev), records, entity_means, noise_bits)
    return pl.pallas_call(
        functools.partial(finish_kernel, float(rec_dev * n)),
        out_shape=(jax.ShapeDtypeStruct((ents, feats), F32), jax.ShapeDtypeStruct((out_rows, width), F32)),
        in_specs=[vspec, vspec],
        out_specs=(vspec, vspec),
    )(new_means, gram)


def sweep(records, owner, entity_means, noise_bits):
    n, na = lax.axis_size("dom"), lax.axis_size("attr")
    rec_dev, feats = records.shape
    sub = 2 * rec_dev // n // na
    out_rows = feats // n
    if na == 4 and n == 8 and sub % 16 == 0 and out_rows == 32:
        return fused(n, na, records, owner, entity_means, noise_bits)
    return shards(records, owner, entity_means, noise_bits)


def solution(mesh):
    in_specs = (P("dom", "attr"), P("dom", None), P("dom", "attr"), P("dom", None))
    out_specs = (P("dom", "attr"), P(("dom", "attr"), None))
    return jax.shard_map(sweep, mesh=mesh, in_specs=in_specs, out_specs=out_specs, check_vma=False)
```

```python
import functools

import jax
import jax.numpy as jnp
from jax import lax
from jax.experimental import pallas as pl
from jax.experimental.pallas import tpu as pltpu
from jax.sharding import PartitionSpec as P


def posterior(raw, bits, live, width):
    uniform = (bits.astype(jnp.float32) + 0.5) / 8192.0
    noise = -jnp.log(-jnp.log(uniform))
    logits = 3.0 * jnp.tanh(raw * width ** (-0.5)) + noise
    expd = jnp.exp(logits)
    return (expd / jnp.sum(expd, axis=1, keepdims=True) * live[:, None]).astype(jnp.bfloat16)


def shards(records, owner, entity_means, noise_bits):
    dom_count = lax.axis_size("dom")
    attr_count = lax.axis_size("attr")
    rec_dev, feat_cols = records.shape
    slot_count = 2 * rec_dev
    capacity = slot_count // dom_count
    width = feat_cols * attr_count
    total_records = rec_dev * dom_count
    dest = owner[:, 0]
    onehot = (dest[:, None] == jnp.arange(dom_count, dtype=jnp.int32)[None, :]).astype(jnp.float32)
    order = jnp.arange(rec_dev, dtype=jnp.int32)
    earlier = (order[:, None] >= order[None, :]).astype(jnp.bfloat16)
    running = jnp.dot(earlier, onehot.astype(jnp.bfloat16), preferred_element_type=jnp.float32)
    rank = jnp.sum(running * onehot, axis=1).astype(jnp.int32) - 1
    position = dest * capacity + rank
    packed = jnp.zeros((slot_count, feat_cols), jnp.bfloat16).at[position].set(records)
    flag_buf = (
        jnp.zeros((slot_count,), jnp.bfloat16).at[position].set(jnp.ones((rec_dev,), jnp.bfloat16))
    )
    arrived, arrived_flags = (
        lax.all_to_all(
            packed.reshape(dom_count, capacity, feat_cols),
            "dom",
            split_axis=0,
            concat_axis=0,
            tiled=True,
        ),
        lax.all_to_all(
            flag_buf.reshape(dom_count, capacity), "dom", split_axis=0, concat_axis=0, tiled=True
        ),
    )
    arrived = arrived.reshape(slot_count, feat_cols)
    live = arrived_flags.reshape(slot_count).astype(jnp.float32)
    raw = lax.psum(jnp.dot(arrived, entity_means.T, preferred_element_type=jnp.float32), "attr")
    weights = posterior(raw, noise_bits, live, width)
    sums_cols = jnp.dot(weights.T, arrived, preferred_element_type=jnp.float32)
    mass_col = jnp.sum(weights.astype(jnp.float32), axis=0)[:, None]
    recon = jnp.dot(weights, entity_means, preferred_element_type=jnp.float32)
    col_resid = ((arrived.astype(jnp.float32) - recon) * live[:, None]).astype(jnp.bfloat16)
    residual = lax.all_to_all(col_resid, "attr", split_axis=0, concat_axis=1, tiled=True)
    new_means = (sums_cols + 1.0 * entity_means.astype(jnp.float32)) / (mass_col + 1.0)
    term = lax.dot_general(
        residual, residual, (((0,), (0,)), ((), ())), preferred_element_type=jnp.float32
    )
    gram = lax.psum_scatter(term / total_records, ("dom", "attr"), scatter_dimension=0, tiled=True)
    return (new_means, gram)

MESH = pl.DeviceIdType.MESH
F32, BF16 = jnp.float32, jnp.bfloat16
GROUP = 2
LANES = 128
TILES = 5
MIRROR = 3
ENDS = (0, 4)


def nt(a, b):
    return lax.dot_general(a, b, (((1,), (1,)), ((), ())), preferred_element_type=F32)


def nn(a, b):
    return jnp.dot(a, b, preferred_element_type=F32)


def remote(src, dst, send_sem, recv_sem, dev):
    return pltpu.make_async_remote_copy(
        src_ref=src, dst_ref=dst, send_sem=send_sem, recv_sem=recv_sem, device_id=dev, device_id_type=MESH
    )


def landed(ref, sem):
    pltpu.make_async_copy(ref, ref, sem).wait()


def sweep_kernel(
    n, na, owner_hbm, records_hbm, means_hbm, noise_ref, new_ref, gram_ref,
    owner_ref, records_ref,
    rank_ref, meta_ref, metas, packed, x_ref, m_ref, bits_ref, gumbel_ref, live_ref, w_ref, wt_ref, r_ref, rt_ref,
    mass_ref, mass_send, masses, diag_ref, diag_send, diags, s_send, s_keep, s_recv, s_send2, s_recv2,
    g_acc, g_send, g_recv, gx_send, gx_recv, gy_send, gy_recv, gz_keep, gz_send, gz_recv, gm_send, gm_recv,
    ez_send, ez_recv, ex_send, ex_recv, ey_send, ey_recv, e_keep, p_ref,
    in_sem, rec_send, rec_recv, meta_send, meta_recv, mean_send, mean_recv, bits_sem,
    mass_ssem, mass_rsem, diag_ssem, diag_rsem, sum_ssem, sum_rsem, gc_ssem, gc_rsem, gx_ssem, gx_rsem, gy_ssem, gy_rsem,
    gz_ssem, gz_rsem, gm_ssem, gm_rsem, ys_ssem, ys_rsem, ez_ssem, ez_rsem, ex_ssem, ex_rsem, ey_ssem, ey_rsem,
):
    rec_dev, feats = records_ref.shape
    ents = m_ref.shape[1]
    cap = 2 * rec_dev // n
    sub = cap // na
    width = feats * na
    d, q = lax.axis_index("dom"), lax.axis_index("attr")
    me = d * na + q
    total = n * na
    x_bit, z = lax.rem(d, 2), d // 2
    c_bit, y_bit = lax.rem(q, 2), q // 2
    nz = n // 2
    rows = GROUP * sub
    out_rows = width // total

    owner_in = pltpu.make_async_copy(owner_hbm, owner_ref, in_sem.at[0])
    records_in = pltpu.make_async_copy(records_hbm, records_ref, in_sem.at[1])
    means_in = pltpu.make_async_copy(means_hbm, m_ref.at[q], in_sem.at[2])
    owner_in.start()
    records_in.start()
    means_in.start()

    barrier = pltpu.get_barrier_semaphore()

    @pl.loop(1, total)
    def _(i):
        dev = lax.rem(me + i, total)
        pl.semaphore_signal(barrier, inc=1, device_id=(dev // na, lax.rem(dev, na)), device_id_type=MESH)

    def bits_copy(s):
        at = pl.ds(pl.multiple_of(s * cap + q * sub, sub), sub)
        return pltpu.make_async_copy(
            noise_ref.at[at, :], bits_ref.at[pl.ds(pl.multiple_of(s * sub, sub), sub), :], bits_sem.at[0]
        )

    @pl.loop(0, n)
    def _(s):
        bits_copy(s).start()

    owner_in.wait()
    blk = 256
    ids = lax.broadcasted_iota(jnp.int32, (n, blk), 0)
    upper = (
        lax.broadcasted_iota(jnp.int32, (blk, blk), 0) <= lax.broadcasted_iota(jnp.int32, (blk, blk), 1)
    ).astype(F32).astype(BF16)
    cuts = [slice(b * blk, (b + 1) * blk) for b in range(rec_dev // blk)]
    hots = [(ids == owner_ref[:, cols]).astype(F32) for cols in cuts]
    runs = nn(jnp.concatenate(hots, axis=0).astype(BF16), upper)
    carry = jnp.zeros((n, 1), F32)
    for b, cols in enumerate(cuts):
        run = runs[b * n:(b + 1) * n, :] + carry
        rank_ref[:, cols] = (jnp.sum(run * hots[b], axis=0, keepdims=True) - 1.0).astype(jnp.int32)
        carry = carry + jnp.sum(hots[b], axis=1, keepdims=True)
    counts = jnp.broadcast_to(carry, (n, LANES)).astype(jnp.int32)
    meta_ref[...] = counts
    metas[d] = counts

    def plane(i):
        far, across, near = lax.rem(z + 2, nz), nz - 1 - z, z + 1 - 2 * lax.rem(z, 2)
        return jnp.where(i == 0, far, jnp.where(i == 1, across, jnp.where(i == 2, z, near)))

    def target(t):
        return plane(t // 2) * 2 + lax.rem(x_bit + t, 2)

    def source_plane(p):
        return plane(lax.rem(p + 2, nz))

    def mean_copy(peer):
        return remote(m_ref.at[q], m_ref.at[q], mean_send.at[0], mean_recv.at[0], (d, peer))

    def meta_copy(o):
        return remote(meta_ref, metas.at[d], meta_send.at[0], meta_recv.at[z], (o, q))

    def rec_copy(t, j, o):
        return remote(
            packed.at[pl.ds(pl.multiple_of(t * cap + j * sub, sub), sub), :],
            x_ref.at[q, pl.ds(pl.multiple_of(d * sub, sub), sub), :],
            rec_send.at[0], rec_recv.at[z], (o, j),
        )

    def pack(t):
        pos = jnp.where(owner_ref[...] == target(t), rank_ref[...], -1)
        hot = (lax.broadcasted_iota(jnp.int32, (cap, rec_dev), 0) == pos).astype(F32).astype(BF16)
        packed[pl.ds(pl.multiple_of(t * cap, cap), cap), :] = nn(hot, records_ref[...]).astype(BF16)

    def dispatch(t):
        o = target(t)
        for j in range(na):
            mine = jnp.logical_and(o == d, q == j)

            @pl.when(jnp.logical_not(mine))
            def _():
                rec_copy(t, j, o).start()

            @pl.when(mine)
            def _():
                x_ref[j, pl.ds(pl.multiple_of(d * sub, sub), sub), :] = (
                    packed[pl.ds(pl.multiple_of(t * cap + j * sub, sub), sub), :]
                )

        @pl.when(o != d)
        def _():
            meta_copy(o).start()

    records_in.wait()
    pack(0)
    means_in.wait()
    pl.semaphore_wait(barrier, total - 1)
    dispatch(0)
    for j in range(1, na):
        mean_copy(lax.rem(q + j, na)).start()

    @pl.loop(1, n)
    def _(t):
        pack(t)
        dispatch(t)

    core_peer, y_peer = q + 1 - 2 * c_bit, lax.rem(q + 2, na)
    x_peer = d + 1 - 2 * x_bit
    order = [(dc, dx, dy) for dc in (1, 0) for dx in (1, 0) for dy in (1, 0)]
    mine = c_bit * 4 + x_bit * 2 + y_bit

    def flip(bit, by):
        return 1 - bit if by else bit

    mass_ref[...] = jnp.zeros_like(mass_ref)
    diag_ref[...] = jnp.zeros_like(diag_ref)
    s_send[...] = jnp.zeros_like(s_send)
    s_keep[...] = jnp.zeros_like(s_keep)
    g_acc[...] = jnp.zeros_like(g_acc)

    landed(m_ref.at[pl.ds(0, na - 1)], mean_recv.at[0])
    landed(bits_ref, bits_sem.at[0])

    @pl.loop(0, n)
    def _(s):
        at = pl.ds(pl.multiple_of(s * sub, sub), sub)
        gumbel_ref[at, :] = 1.0 / (-jnp.log((bits_ref[at, :].astype(F32) + 0.5) / 8192.0))

    def weigh(p):
        zs = source_plane(p)

        @pl.when(zs == z)
        def _():
            landed(metas.at[pl.ds(0, GROUP - 1)], meta_recv.at[zs])
            landed(packed.at[pl.ds(0, (GROUP * na - 1) * sub), :], rec_recv.at[zs])

        @pl.when(zs != z)
        def _():
            landed(metas.at[pl.ds(0, GROUP)], meta_recv.at[zs])
            landed(packed.at[pl.ds(0, GROUP * na * sub), :], rec_recv.at[zs])

        at = pl.ds(pl.multiple_of(zs * rows, rows), rows)
        raw = nt(x_ref[0, at, :], m_ref[0])
        for a in range(1, na):
            raw = raw + nt(x_ref[a, at, :], m_ref[a])
        expd = jnp.exp(3.0 * jnp.tanh(raw * width ** (-0.5))) * gumbel_ref[at, :]
        row = lax.broadcasted_iota(jnp.int32, (rows, 1), 0)
        live = jnp.zeros((rows, 1), F32)
        for t in range(GROUP):
            cnt = metas[zs * GROUP + t, pl.ds(d, 1), :][:, :1]
            inside = jnp.logical_and(row >= t * sub, row < (t + 1) * sub)
            live = live + jnp.where(jnp.logical_and(inside, row - t * sub + q * sub < cnt), 1.0, 0.0)
        w = (expd * (live / jnp.sum(expd, axis=1, keepdims=True))).astype(BF16)
        w_ref[...] = w
        live_ref[...] = jnp.broadcast_to(live, live_ref.shape)
        mass_ref[...] += jnp.broadcast_to(jnp.sum(w.astype(F32), axis=0, keepdims=True), mass_ref.shape)
        for b in range(ents // LANES):
            cols = slice(b * LANES, (b + 1) * LANES)
            wt_ref[cols, :] = w_ref[:, cols].T

    def residual(p):
        at = pl.ds(pl.multiple_of(source_plane(p) * rows, rows), rows)
        w, live = w_ref[...], live_ref[:, :1]
        for a in range(na):
            recon = nn(w, m_ref[a])
            res = ((x_ref[a, at, :].astype(F32) - recon) * live).astype(BF16)
            r_ref[:, a * feats:(a + 1) * feats] = res
            wide = res.astype(F32)
            square = jnp.sum(wide * wide, axis=0, keepdims=True)
            diag_ref[:, a * feats:(a + 1) * feats] += jnp.broadcast_to(square, (8, feats))
        for b in range(n):
            turned = r_ref[:, b * LANES:(b + 1) * LANES].T
            zz, xx = b // 2, b % 2
            for e in range(na):
                g = (e % 2) * 4 + xx * 2 + e // 2
                piece = turned[e * out_rows:(e + 1) * out_rows, :]
                for copy in (g, g + 8):
                    if copy < 8 + TILES - 1:
                        rt_ref[pl.ds(copy * LANES + zz * out_rows, out_rows), :] = piece

    def partial_sums(p, t, core):
        at = pl.ds(pl.multiple_of(source_plane(p) * rows, rows), rows)
        return nn(wt_ref[...], x_ref[(y_bit if t == 0 else 1 - y_bit) * 2 + core, at, :])

    def band(k):
        dc, dx, dy = order[k]
        return flip(c_bit, dc) * 4 + flip(x_bit, dx) * 2 + flip(y_bit, dy)

    def gram_band(k):
        first = pl.multiple_of(band(k) * LANES, LANES)
        return nt(rt_ref[pl.ds(first, LANES), :], rt_ref[pl.ds(first, TILES * LANES), :])

    def add_gram(k):
        new = gram_band(k)
        for m in range(TILES):
            g_acc[m, k * LANES:(k + 1) * LANES, :] += new[:, m * LANES:(m + 1) * LANES]

    @pl.loop(0, nz - 1)
    def _(p):
        weigh(p)
        residual(p)
        for t in range(2):
            s_send[t] += partial_sums(p, t, 1 - c_bit)
            s_keep[t] += partial_sums(p, t, c_bit)
        for k in range(8):
            add_gram(k)

    def mass_copy(peer):
        return remote(mass_send, masses.at[q], mass_ssem.at[0], mass_rsem.at[0], (d, peer))

    def diag_copy(j):
        dev = lax.rem(me + j, total)
        return remote(
            diag_send.at[dev // na], diags.at[j], diag_ssem.at[0], diag_rsem.at[0], (dev // na, lax.rem(dev, na))
        )

    def core_sums(t):
        return remote(s_send.at[t], s_recv.at[t], sum_ssem.at[0], sum_rsem.at[t], (d, core_peer))

    def y_sums():
        return remote(s_send2, s_recv2, ys_ssem.at[0], ys_rsem.at[0], (d, y_peer))

    def core_gram(m):
        return remote(g_send.at[m], g_recv.at[m], gc_ssem.at[0], gc_rsem.at[m], (d, core_peer))

    def x_gram(m):
        return remote(gx_send.at[m - 1], gx_recv.at[m - 1], gx_ssem.at[0], gx_rsem.at[m - 1], (x_peer, q))

    def y_gram(m):
        return remote(gy_send.at[m - 1], gy_recv.at[m - 1], gy_ssem.at[0], gy_rsem.at[m - 1], (d, y_peer))

    def z_copy(m, j):
        to = lax.rem(z + j, nz)
        return remote(
            gz_send.at[m - 1, pl.ds(pl.multiple_of(to * out_rows, out_rows), out_rows), :],
            gz_recv.at[j - 1, m - 1], gz_ssem.at[0], gz_rsem.at[0], (to * 2 + x_bit, q),
        )

    def mirror_copy(m, to):
        g = lax.rem(mine + m, 8)
        return remote(
            gm_send.at[m - 1, pl.ds(to * out_rows, out_rows), :],
            gm_recv.at[z, m - 1], gm_ssem.at[0], gm_rsem.at[0],
            (to * 2 + lax.rem(g // 2, 2), lax.rem(g, 2) * 2 + g // 4),
        )

    def ends_z(e, j):
        to = lax.rem(z + j, nz)
        return remote(
            ez_send.at[e, to], ez_recv.at[e, j - 1], ez_ssem.at[0], ez_rsem.at[e], (to * 2 + x_bit, q)
        )

    def ends_x(e):
        return remote(ex_send.at[e], ex_recv.at[e], ex_ssem.at[0], ex_rsem.at[e], (x_peer, q))

    def ends_y(e):
        return remote(ey_send.at[e], ey_recv.at[e], ey_ssem.at[0], ey_rsem.at[0], (d, y_peer))

    half, quart, eighth = 4 * LANES, 6 * LANES, 7 * LANES

    def to_x(m):
        core_gram(m).wait_recv()
        gx_send[m - 1] = (g_acc[m, half:quart, :] + g_recv[m, :2 * LANES, :].astype(F32)).astype(BF16)
        x_gram(m).start()
        g_acc[m, quart:, :] += g_recv[m, 2 * LANES:, :].astype(F32)

    def to_y(m):
        x_gram(m).wait_recv()
        gy_send[m - 1] = (g_acc[m, quart:eighth, :] + gx_recv[m - 1, :LANES, :].astype(F32)).astype(BF16)
        y_gram(m).start()
        g_acc[m, eighth:, :] += gx_recv[m - 1, LANES:, :].astype(F32)

    def to_z(m):
        y_gram(m).wait_recv()
        full = g_acc[m, eighth:, :] + gy_recv[m - 1].astype(F32)
        gz_send[m - 1] = full.astype(BF16)
        for j in range(1, nz):
            z_copy(m, j).start()
        gm_send[m - 1] = full.T.astype(BF16)
        for to in range(nz):
            mirror_copy(m, to).start()
        gz_keep[m - 1] = full

    def ends_to_z(e):
        m = ENDS[e]
        core_gram(m).wait_recv()
        full = g_acc[m, half:, :] + g_recv[m].astype(F32)
        narrow = full.astype(BF16)
        for k in range(4):
            for zz in range(nz):
                first = k * LANES + zz * out_rows
                ez_send[e, zz, k * out_rows:(k + 1) * out_rows, :] = narrow[first:first + out_rows, :]
        for j in range(1, nz):
            ends_z(e, j).start()
        g_acc[m, half:, :] = full

    def ends_to_x(e):
        landed(ez_recv.at[e], ez_rsem.at[e])
        for k in range(4):
            rows_k = slice(k * out_rows, (k + 1) * out_rows)
            first = pl.multiple_of(half + k * LANES + z * out_rows, out_rows)
            acc = g_acc[ENDS[e], pl.ds(first, out_rows), :]
            for j in range(1, nz):
                acc = acc + ez_recv[e, j - 1, rows_k, :].astype(F32)
            if k < 2:
                ex_send[e, rows_k, :] = acc.astype(BF16)
            else:
                e_keep[e, (k - 2) * out_rows:(k - 1) * out_rows, :] = acc
        ends_x(e).start()

    def ends_to_y(e):
        ends_x(e).wait_recv()
        ey_send[e] = (e_keep[e, :out_rows, :] + ex_recv[e, :out_rows, :].astype(F32)).astype(BF16)
        ends_y(e).start()
        e_keep[e, out_rows:, :] += ex_recv[e, out_rows:, :].astype(F32)

    final = nz - 1
    weigh(final)
    s_send[1] += partial_sums(final, 1, 1 - c_bit)
    core_sums(1).start()
    residual(final)
    for k in range(4):
        new = gram_band(k)
        for m in range(TILES):
            at = slice(k * LANES, (k + 1) * LANES)
            g_send[m, at, :] = (g_acc[m, at, :] + new[:, m * LANES:(m + 1) * LANES]).astype(BF16)
    for m in (1, ENDS[0], 2, ENDS[1], 3):
        core_gram(m).start()
    s_keep[1] += partial_sums(final, 1, c_bit)
    core_sums(1).wait_recv()
    s_send2[...] = (s_keep[1] + s_recv[1]).astype(BF16)
    y_sums().start()
    for k in range(4, 8):
        add_gram(k)
    to_x(1)
    ends_to_z(0)
    to_x(2)
    ends_to_z(1)
    to_x(3)
    s_send[0] += partial_sums(final, 0, 1 - c_bit)
    core_sums(0).start()
    mass_send[...] = mass_ref[:1, :]
    masses[q] = mass_ref[:1, :]
    for j in range(1, na):
        mass_copy(lax.rem(q + j, na)).start()
    for b in range(n):
        diag_send[b] = diag_ref[:1, b * LANES:(b + 1) * LANES]
    diags[0] = diag_send[d]

    @pl.loop(1, total)
    def _(j):
        diag_copy(j).start()

    s_keep[0] += partial_sums(final, 0, c_bit)
    to_y(1)
    to_y(2)
    to_y(3)
    ends_to_x(0)
    to_z(1)
    to_z(2)
    ends_to_x(1)
    to_z(3)
    ends_to_y(0)
    ends_to_y(1)

    core_sums(0).wait_recv()
    landed(masses.at[pl.ds(0, na - 1)], mass_rsem.at[0])
    landed(s_recv2, ys_rsem.at[0])
    mass = masses[0]
    for a in range(1, na):
        mass = mass + masses[a]
    col = jnp.broadcast_to(mass, (LANES, ents)).T
    for b in range(feats // LANES):
        cols = slice(b * LANES, (b + 1) * LANES)
        full = s_keep[0, :, cols] + s_recv[0, :, cols] + s_recv2[:, cols].astype(F32)
        new_ref[:, cols] = (full + 1.0 * m_ref[q, :, cols].astype(F32)) / (col + 1.0)

    landed(diags.at[pl.ds(1, total - 1)], diag_rsem.at[0])
    diag = jnp.broadcast_to(jnp.sum(diags[...], axis=0), (out_rows, LANES))
    row = lax.broadcasted_iota(jnp.int32, (out_rows, LANES), 0)
    lane = lax.broadcasted_iota(jnp.int32, (out_rows, LANES), 1)
    diag = jnp.sum(jnp.where(lane == row + q * out_rows, diag, 0.0), axis=1, keepdims=True)
    own_rows = pl.ds(pl.multiple_of(z * out_rows, out_rows), out_rows)
    landed(ey_recv, ey_rsem.at[0])
    for e, m in enumerate(ENDS):
        acc = e_keep[e, out_rows:, :] + ey_recv[e].astype(F32)
        if m == 0:
            acc = jnp.where(lane == row + z * out_rows, diag, acc)
        p_ref[lax.rem(mine + m, 8)] = acc
    landed(gz_recv, gz_rsem.at[0])
    for m in range(1, MIRROR + 1):
        acc = gz_keep[m - 1, own_rows, :]
        for j in range(1, nz):
            acc = acc + gz_recv[j - 1, m - 1].astype(F32)
        p_ref[lax.rem(mine + m, 8)] = acc
    landed(gm_recv, gm_rsem.at[0])
    for m in range(1, MIRROR + 1):
        acc = jnp.zeros((out_rows, LANES), F32)
        for zz in range(nz):
            acc = acc + gm_recv[zz, m - 1].astype(F32)
        p_ref[lax.rem(mine + 8 - m, 8)] = acc
    for b in range(n):
        zz, xx = b // 2, b % 2
        gram_ref[:, b * LANES:(b + 1) * LANES] = jnp.concatenate(
            [
                p_ref[(e % 2) * 4 + xx * 2 + e // 2, :, zz * out_rows:(zz + 1) * out_rows]
                for e in range(na)
            ],
            axis=1,
        ) / float(rec_dev * n)

    landed(m_ref.at[pl.ds(0, na - 1)], mean_send.at[0])
    landed(masses.at[pl.ds(0, na - 1)], mass_ssem.at[0])
    landed(s_send, sum_ssem.at[0])
    landed(s_send2, ys_ssem.at[0])
    landed(diags.at[pl.ds(1, total - 1)], diag_ssem.at[0])
    landed(g_send, gc_ssem.at[0])
    landed(gx_send, gx_ssem.at[0])
    landed(gy_send, gy_ssem.at[0])
    landed(gz_recv, gz_ssem.at[0])
    landed(gm_recv, gm_ssem.at[0])
    landed(ez_recv, ez_ssem.at[0])
    landed(ex_recv, ex_ssem.at[0])
    landed(ey_recv, ey_ssem.at[0])
    landed(metas.at[pl.ds(0, n - 1)], meta_send.at[0])
    landed(packed.at[pl.ds(0, (total - 1) * sub), :], rec_send.at[0])

def finish_kernel(means_ref, gram_ref, means_out, gram_out, sems):
    step = means_ref.shape[0] // 4
    copies = [
        pltpu.make_async_copy(
            means_ref.at[pl.ds(c * step, step)], means_out.at[pl.ds(c * step, step)], sems.at[c]
        )
        for c in range(4)
    ] + [pltpu.make_async_copy(gram_ref, gram_out, sems.at[4])]
    for copy in copies:
        copy.start()
    for copy in copies:
        copy.wait()


def fused(n, na, records, owner, entity_means, noise_bits):
    rec_dev, feats = records.shape
    ents = entity_means.shape[0]
    cap = 2 * rec_dev // n
    slots = 2 * rec_dev // na
    rows = GROUP * (cap // na)
    width = feats * na
    total = n * na
    out_rows = width // total
    nz = n // 2
    vm, dma = pltpu.VMEM, pltpu.SemaphoreType.DMA
    vspec = pl.BlockSpec(memory_space=pltpu.VMEM)
    hspec = pl.BlockSpec(memory_space=pl.ANY)
    scratch = [
        vm((1, rec_dev), jnp.int32), vm((rec_dev, feats), BF16),
        vm((1, rec_dev), jnp.int32), vm((n, LANES), jnp.int32), vm((n, n, LANES), jnp.int32),
        vm((n * cap, feats), BF16), vm((na, slots, feats), BF16), vm((na, ents, feats), BF16),
        vm((slots, ents), jnp.int32), vm((slots, ents), F32), vm((rows, LANES), F32), vm((rows, ents), BF16), vm((ents, rows), BF16),
        vm((rows, width), BF16), vm(((8 + TILES - 1) * LANES, rows), BF16),
        vm((8, ents), F32), vm((1, ents), F32), vm((na, 1, ents), F32),
        vm((8, width), F32), vm((n, 1, LANES), F32), vm((total, 1, LANES), F32),
        vm((2, ents, feats), F32), vm((2, ents, feats), F32), vm((2, ents, feats), F32),
        vm((ents, feats), BF16), vm((ents, feats), BF16),
        vm((TILES, 8 * LANES, LANES), F32),
        vm((TILES, 4 * LANES, LANES), BF16), vm((TILES, 4 * LANES, LANES), BF16),
        vm((MIRROR, 2 * LANES, LANES), BF16), vm((MIRROR, 2 * LANES, LANES), BF16),
        vm((MIRROR, LANES, LANES), BF16), vm((MIRROR, LANES, LANES), BF16),
        vm((MIRROR, LANES, LANES), F32), vm((MIRROR, LANES, LANES), BF16),
        vm((nz - 1, MIRROR, out_rows, LANES), BF16),
        vm((MIRROR, LANES, LANES), BF16), vm((nz, MIRROR, out_rows, LANES), BF16),
        vm((2, nz, LANES, LANES), BF16), vm((2, nz - 1, LANES, LANES), BF16),
        vm((2, 2 * out_rows, LANES), BF16), vm((2, 2 * out_rows, LANES), BF16),
        vm((2, out_rows, LANES), BF16), vm((2, out_rows, LANES), BF16), vm((2, 2 * out_rows, LANES), F32),
        vm((8, out_rows, LANES), F32),
        dma((3,)),
        dma((1,)), dma((nz,)), dma((1,)), dma((nz,)), *(dma((1,)) for _ in range(7)),
        dma((1,)), dma((2,)), *(dma((size,)) for size in (1, TILES, 1, MIRROR, 1, MIRROR)),
        *(dma((1,)) for _ in range(6)), *(dma((size,)) for size in (1, 2, 1, 2, 1, 1)),
    ]
    new_means, gram = pl.pallas_call(
        functools.partial(sweep_kernel, n, na),
        out_shape=(vm((ents, feats), F32), vm((out_rows, width), F32)),
        in_specs=[hspec, hspec, hspec, hspec],
        out_specs=(vspec, vspec),
        scratch_shapes=scratch,
        compiler_params=pltpu.CompilerParams(
            collective_id=0, has_side_effects=True, vmem_limit_bytes=56 * 1024 * 1024
        ),
    )(owner.reshape(1, rec_dev), records, entity_means, noise_bits)
    return pl.pallas_call(
        finish_kernel,
        out_shape=(jax.ShapeDtypeStruct((ents, feats), F32), jax.ShapeDtypeStruct((out_rows, width), F32)),
        in_specs=[vspec, vspec],
        out_specs=(hspec, hspec),
        scratch_shapes=[dma((5,))],
    )(pltpu.with_memory_space_constraint(new_means, pltpu.VMEM), pltpu.with_memory_space_constraint(gram, pltpu.VMEM))


def sweep(records, owner, entity_means, noise_bits):
    n, na = lax.axis_size("dom"), lax.axis_size("attr")
    rec_dev, feats = records.shape
    sub = 2 * rec_dev // n // na
    out_rows = feats // n
    if na == 4 and n == 8 and sub % 16 == 0 and out_rows == 32:
        return fused(n, na, records, owner, entity_means, noise_bits)
    return shards(records, owner, entity_means, noise_bits)


def solution(mesh):
    in_specs = (P("dom", "attr"), P("dom", None), P("dom", "attr"), P("dom", None))
    out_specs = (P("dom", "attr"), P(("dom", "attr"), None))
    return jax.shard_map(sweep, mesh=mesh, in_specs=in_specs, out_specs=out_specs, check_vma=False)
```

```python
import functools

import jax
import jax.numpy as jnp
from jax import lax
from jax.experimental import pallas as pl
from jax.experimental.pallas import tpu as pltpu
from jax.sharding import PartitionSpec as P


def posterior(raw, bits, live, width):
    uniform = (bits.astype(jnp.float32) + 0.5) / 8192.0
    noise = -jnp.log(-jnp.log(uniform))
    logits = 3.0 * jnp.tanh(raw * width ** (-0.5)) + noise
    expd = jnp.exp(logits)
    return (expd / jnp.sum(expd, axis=1, keepdims=True) * live[:, None]).astype(jnp.bfloat16)


def shards(records, owner, entity_means, noise_bits):
    dom_count = lax.axis_size("dom")
    attr_count = lax.axis_size("attr")
    rec_dev, feat_cols = records.shape
    slot_count = 2 * rec_dev
    capacity = slot_count // dom_count
    width = feat_cols * attr_count
    total_records = rec_dev * dom_count
    dest = owner[:, 0]
    onehot = (dest[:, None] == jnp.arange(dom_count, dtype=jnp.int32)[None, :]).astype(jnp.float32)
    order = jnp.arange(rec_dev, dtype=jnp.int32)
    earlier = (order[:, None] >= order[None, :]).astype(jnp.bfloat16)
    running = jnp.dot(earlier, onehot.astype(jnp.bfloat16), preferred_element_type=jnp.float32)
    rank = jnp.sum(running * onehot, axis=1).astype(jnp.int32) - 1
    position = dest * capacity + rank
    packed = jnp.zeros((slot_count, feat_cols), jnp.bfloat16).at[position].set(records)
    flag_buf = (
        jnp.zeros((slot_count,), jnp.bfloat16).at[position].set(jnp.ones((rec_dev,), jnp.bfloat16))
    )
    arrived, arrived_flags = (
        lax.all_to_all(
            packed.reshape(dom_count, capacity, feat_cols),
            "dom",
            split_axis=0,
            concat_axis=0,
            tiled=True,
        ),
        lax.all_to_all(
            flag_buf.reshape(dom_count, capacity), "dom", split_axis=0, concat_axis=0, tiled=True
        ),
    )
    arrived = arrived.reshape(slot_count, feat_cols)
    live = arrived_flags.reshape(slot_count).astype(jnp.float32)
    raw = lax.psum(jnp.dot(arrived, entity_means.T, preferred_element_type=jnp.float32), "attr")
    weights = posterior(raw, noise_bits, live, width)
    sums_cols = jnp.dot(weights.T, arrived, preferred_element_type=jnp.float32)
    mass_col = jnp.sum(weights.astype(jnp.float32), axis=0)[:, None]
    recon = jnp.dot(weights, entity_means, preferred_element_type=jnp.float32)
    col_resid = ((arrived.astype(jnp.float32) - recon) * live[:, None]).astype(jnp.bfloat16)
    residual = lax.all_to_all(col_resid, "attr", split_axis=0, concat_axis=1, tiled=True)
    new_means = (sums_cols + 1.0 * entity_means.astype(jnp.float32)) / (mass_col + 1.0)
    term = lax.dot_general(
        residual, residual, (((0,), (0,)), ((), ())), preferred_element_type=jnp.float32
    )
    gram = lax.psum_scatter(term / total_records, ("dom", "attr"), scatter_dimension=0, tiled=True)
    return (new_means, gram)

MESH = pl.DeviceIdType.MESH
F32, BF16 = jnp.float32, jnp.bfloat16
GROUP = 2
LANES = 128
TILES = 5
MIRROR = 3
ENDS = (0, 4)


def nt(a, b):
    return lax.dot_general(a, b, (((1,), (1,)), ((), ())), preferred_element_type=F32)


def nn(a, b):
    return jnp.dot(a, b, preferred_element_type=F32)


def remote(src, dst, send_sem, recv_sem, dev):
    return pltpu.make_async_remote_copy(
        src_ref=src, dst_ref=dst, send_sem=send_sem, recv_sem=recv_sem, device_id=dev, device_id_type=MESH
    )


def landed(ref, sem):
    pltpu.make_async_copy(ref, ref, sem).wait()


def sweep_kernel(
    n, na, owner_hbm, records_hbm, means_hbm, noise_ref, new_ref, gram_ref,
    owner_ref, records_ref,
    rank_ref, meta_ref, metas, packed, x_ref, m_ref, bits_ref, gumbel_ref, live_ref, w_ref, wt_ref, r_ref, rt_ref,
    mass_ref, mass_send, masses, diag_ref, diag_send, diags, s_send, s_keep, s_recv, s_send2, s_recv2,
    g_acc, g_send, g_recv, gx_send, gx_recv, gy_send, gy_recv, gz_keep, gz_send, gz_recv, gm_send, gm_recv,
    ez_send, ez_recv, ep_send, ep_recv, e_keep, p_ref,
    in_sem, rec_send, rec_recv, meta_send, meta_recv, mean_send, mean_recv, bits_sem,
    mass_ssem, mass_rsem, diag_ssem, diag_rsem, sum_ssem, sum_rsem, gc_ssem, gc_rsem, gx_ssem, gx_rsem, gy_ssem, gy_rsem,
    gz_ssem, gz_rsem, gm_ssem, gm_rsem, ys_ssem, ys_rsem, ez_ssem, ez_rsem, ep_ssem, ep_rsem,
):
    rec_dev, feats = records_ref.shape
    ents = m_ref.shape[1]
    cap = 2 * rec_dev // n
    sub = cap // na
    width = feats * na
    d, q = lax.axis_index("dom"), lax.axis_index("attr")
    me = d * na + q
    total = n * na
    x_bit, z = lax.rem(d, 2), d // 2
    c_bit, y_bit = lax.rem(q, 2), q // 2
    nz = n // 2
    rows = GROUP * sub
    out_rows = width // total
    inner = lax.rem((z + 1) // 2, 2)

    owner_in = pltpu.make_async_copy(owner_hbm, owner_ref, in_sem.at[0])
    records_in = pltpu.make_async_copy(records_hbm, records_ref, in_sem.at[1])
    means_in = pltpu.make_async_copy(means_hbm, m_ref.at[q], in_sem.at[2])
    owner_in.start()
    records_in.start()
    means_in.start()

    barrier = pltpu.get_barrier_semaphore()

    @pl.loop(1, total)
    def _(i):
        dev = lax.rem(me + i, total)
        pl.semaphore_signal(barrier, inc=1, device_id=(dev // na, lax.rem(dev, na)), device_id_type=MESH)

    def bits_copy(s):
        at = pl.ds(pl.multiple_of(s * cap + q * sub, sub), sub)
        return pltpu.make_async_copy(
            noise_ref.at[at, :], bits_ref.at[pl.ds(pl.multiple_of(s * sub, sub), sub), :], bits_sem.at[0]
        )

    @pl.loop(0, n)
    def _(s):
        bits_copy(s).start()

    owner_in.wait()
    blk = 256
    ids = lax.broadcasted_iota(jnp.int32, (n, blk), 0)
    upper = (
        lax.broadcasted_iota(jnp.int32, (blk, blk), 0) <= lax.broadcasted_iota(jnp.int32, (blk, blk), 1)
    ).astype(F32).astype(BF16)
    cuts = [slice(b * blk, (b + 1) * blk) for b in range(rec_dev // blk)]
    hots = [(ids == owner_ref[:, cols]).astype(F32) for cols in cuts]
    runs = nn(jnp.concatenate(hots, axis=0).astype(BF16), upper)
    carry = jnp.zeros((n, 1), F32)
    for b, cols in enumerate(cuts):
        run = runs[b * n:(b + 1) * n, :] + carry
        rank_ref[:, cols] = (jnp.sum(run * hots[b], axis=0, keepdims=True) - 1.0).astype(jnp.int32)
        carry = carry + jnp.sum(hots[b], axis=1, keepdims=True)
    counts = jnp.broadcast_to(carry, (n, LANES)).astype(jnp.int32)
    meta_ref[...] = counts
    metas[d] = counts

    def plane(i):
        far, across, near = lax.rem(z + 2, nz), nz - 1 - z, z + 1 - 2 * lax.rem(z, 2)
        return jnp.where(i == 0, far, jnp.where(i == 1, across, jnp.where(i == 2, z, near)))

    def target(t):
        return plane(t // 2) * 2 + lax.rem(x_bit + t, 2)

    def source_plane(p):
        outer = jnp.where(p == 0, 1, jnp.where(p == 1, 2, jnp.where(p == 2, 0, 3)))
        return plane(jnp.where(inner == 1, lax.rem(p + 2, nz), outer))

    def mean_copy(peer):
        return remote(m_ref.at[q], m_ref.at[q], mean_send.at[0], mean_recv.at[0], (d, peer))

    def meta_copy(o):
        return remote(meta_ref, metas.at[d], meta_send.at[0], meta_recv.at[d], (o, q))

    def rec_copy(t, j, o):
        return remote(
            packed.at[pl.ds(pl.multiple_of(t * cap + j * sub, sub), sub), :],
            x_ref.at[q, pl.ds(pl.multiple_of(d * sub, sub), sub), :],
            rec_send.at[0], rec_recv.at[d], (o, j),
        )

    def pack(t):
        pos = jnp.where(owner_ref[...] == target(t), rank_ref[...], -1)
        hot = (lax.broadcasted_iota(jnp.int32, (cap, rec_dev), 0) == pos).astype(F32).astype(BF16)
        packed[pl.ds(pl.multiple_of(t * cap, cap), cap), :] = nn(hot, records_ref[...]).astype(BF16)

    def dispatch(t):
        o = target(t)
        for j in range(na):
            mine = jnp.logical_and(o == d, q == j)

            @pl.when(jnp.logical_not(mine))
            def _():
                rec_copy(t, j, o).start()

            @pl.when(mine)
            def _():
                x_ref[j, pl.ds(pl.multiple_of(d * sub, sub), sub), :] = (
                    packed[pl.ds(pl.multiple_of(t * cap + j * sub, sub), sub), :]
                )

        @pl.when(o != d)
        def _():
            meta_copy(o).start()

    records_in.wait()
    pack(0)
    means_in.wait()
    pl.semaphore_wait(barrier, total - 1)
    dispatch(0)
    for j in range(1, na):
        mean_copy(lax.rem(q + j, na)).start()

    @pl.loop(1, n)
    def _(t):
        pack(t)
        dispatch(t)

    core_peer, y_peer = q + 1 - 2 * c_bit, lax.rem(q + 2, na)
    x_peer = d + 1 - 2 * x_bit
    order = [(dc, dx, dy) for dc in (1, 0) for dx in (1, 0) for dy in (1, 0)]
    mine = c_bit * 4 + x_bit * 2 + y_bit

    def flip(bit, by):
        return 1 - bit if by else bit

    mass_ref[...] = jnp.zeros_like(mass_ref)
    diag_ref[...] = jnp.zeros_like(diag_ref)
    s_send[...] = jnp.zeros_like(s_send)
    s_keep[...] = jnp.zeros_like(s_keep)
    g_acc[...] = jnp.zeros_like(g_acc)

    landed(m_ref.at[pl.ds(0, na - 1)], mean_recv.at[0])
    landed(bits_ref, bits_sem.at[0])

    @pl.loop(0, n)
    def _(s):
        at = pl.ds(pl.multiple_of(s * sub, sub), sub)
        gumbel_ref[at, :] = 1.0 / (-jnp.log((bits_ref[at, :].astype(F32) + 0.5) / 8192.0))

    def arrive(s):
        @pl.when(s == d)
        def _():
            landed(packed.at[pl.ds(0, (na - 1) * sub), :], rec_recv.at[s])

        @pl.when(s != d)
        def _():
            landed(metas.at[pl.ds(0, 1)], meta_recv.at[s])
            landed(packed.at[pl.ds(0, na * sub), :], rec_recv.at[s])

    def weigh(first, count):
        size = count * sub
        for t in range(count):
            arrive(first + t)
        at = pl.ds(pl.multiple_of(first * sub, sub), size)
        raw = nt(x_ref[0, at, :], m_ref[0])
        for a in range(1, na):
            raw = raw + nt(x_ref[a, at, :], m_ref[a])
        expd = jnp.exp(3.0 * jnp.tanh(raw * width ** (-0.5))) * gumbel_ref[at, :]
        row = lax.broadcasted_iota(jnp.int32, (size, 1), 0)
        live = jnp.zeros((size, 1), F32)
        for t in range(count):
            cnt = metas[first + t, pl.ds(d, 1), :][:, :1]
            inside = jnp.logical_and(row >= t * sub, row < (t + 1) * sub)
            live = live + jnp.where(jnp.logical_and(inside, row - t * sub + q * sub < cnt), 1.0, 0.0)
        w = (expd * (live / jnp.sum(expd, axis=1, keepdims=True))).astype(BF16)
        w_ref[:size, :] = w
        live_ref[:size, :] = jnp.broadcast_to(live, (size, LANES))
        mass_ref[...] += jnp.broadcast_to(jnp.sum(w.astype(F32), axis=0, keepdims=True), mass_ref.shape)
        for b in range(ents // LANES):
            cols = slice(b * LANES, (b + 1) * LANES)
            wt_ref[cols, :size] = w_ref[:size, cols].T

    def residual(first, count):
        size = count * sub
        at = pl.ds(pl.multiple_of(first * sub, sub), size)
        w, live = w_ref[:size, :], live_ref[:size, :1]
        for a in range(na):
            recon = nn(w, m_ref[a])
            res = ((x_ref[a, at, :].astype(F32) - recon) * live).astype(BF16)
            r_ref[:size, a * feats:(a + 1) * feats] = res
            wide = res.astype(F32)
            square = jnp.sum(wide * wide, axis=0, keepdims=True)
            diag_ref[:, a * feats:(a + 1) * feats] += jnp.broadcast_to(square, (8, feats))
        for b in range(n):
            turned = r_ref[:size, b * LANES:(b + 1) * LANES].T
            zz, xx = b // 2, b % 2
            for e in range(na):
                g = (e % 2) * 4 + xx * 2 + e // 2
                piece = turned[e * out_rows:(e + 1) * out_rows, :]
                for copy in (g, g + 8):
                    if copy < 8 + TILES - 1:
                        rt_ref[pl.ds(copy * LANES + zz * out_rows, out_rows), :size] = piece

    def partial_sums(first, count, t, core):
        at = pl.ds(pl.multiple_of(first * sub, sub), count * sub)
        return nn(wt_ref[:, :count * sub], x_ref[(y_bit if t == 0 else 1 - y_bit) * 2 + core, at, :])

    def band(k):
        dc, dx, dy = order[k]
        return flip(c_bit, dc) * 4 + flip(x_bit, dx) * 2 + flip(y_bit, dy)

    def gram_band(k, count):
        first, size = pl.multiple_of(band(k) * LANES, LANES), count * sub
        return nt(rt_ref[pl.ds(first, LANES), :size], rt_ref[pl.ds(first, TILES * LANES), :size])

    def add_gram(k, count):
        new = gram_band(k, count)
        for m in range(TILES):
            g_acc[m, k * LANES:(k + 1) * LANES, :] += new[:, m * LANES:(m + 1) * LANES]

    def gather(first, count):
        weigh(first, count)
        residual(first, count)
        for t in range(2):
            s_send[t] += partial_sums(first, count, t, 1 - c_bit)
            s_keep[t] += partial_sums(first, count, t, c_bit)
        for k in range(8):
            add_gram(k, count)

    @pl.loop(0, nz - 1)
    def _(p):
        gather(source_plane(p) * GROUP, GROUP)

    def mass_copy(peer):
        return remote(mass_send, masses.at[q], mass_ssem.at[0], mass_rsem.at[0], (d, peer))

    def diag_copy(j):
        dev = lax.rem(me + j, total)
        return remote(
            diag_send.at[dev // na], diags.at[j], diag_ssem.at[0], diag_rsem.at[0], (dev // na, lax.rem(dev, na))
        )

    def core_sums(t):
        return remote(s_send.at[t], s_recv.at[t], sum_ssem.at[0], sum_rsem.at[t], (d, core_peer))

    def y_sums(first, count):
        at = pl.ds(first * LANES, count * LANES)
        return remote(s_send2.at[at], s_recv2.at[at], ys_ssem.at[0], ys_rsem.at[0], (d, y_peer))

    def core_gram(m):
        return remote(g_send.at[m], g_recv.at[m], gc_ssem.at[0], gc_rsem.at[m], (d, core_peer))

    def x_gram(m):
        return remote(gx_send.at[m - 1], gx_recv.at[m - 1], gx_ssem.at[0], gx_rsem.at[m - 1], (x_peer, q))

    def y_gram(m):
        return remote(gy_send.at[m - 1], gy_recv.at[m - 1], gy_ssem.at[0], gy_rsem.at[m - 1], (d, y_peer))

    def z_copy(m, j):
        to = lax.rem(z + j, nz)
        return remote(
            gz_send.at[m - 1, pl.ds(pl.multiple_of(to * out_rows, out_rows), out_rows), :],
            gz_recv.at[j - 1, m - 1], gz_ssem.at[0], gz_rsem.at[0], (to * 2 + x_bit, q),
        )

    def mirror_copy(m, to):
        g = lax.rem(mine + m, 8)
        return remote(
            gm_send.at[m - 1, pl.ds(to * out_rows, out_rows), :],
            gm_recv.at[z, m - 1], gm_ssem.at[0], gm_rsem.at[0],
            (to * 2 + lax.rem(g // 2, 2), lax.rem(g, 2) * 2 + g // 4),
        )

    def ends_z(e, j):
        to = lax.rem(z + j, nz)
        return remote(
            ez_send.at[e, to], ez_recv.at[e, j - 1], ez_ssem.at[0], ez_rsem.at[e], (to * 2 + x_bit, q)
        )

    def ends_p(e, k):
        return remote(
            ep_send.at[e, k], ep_recv.at[e, k], ep_ssem.at[0], ep_rsem.at[0],
            ((x_peer, y_peer), (x_peer, q), (d, y_peer))[k],
        )

    half, quart, eighth = 4 * LANES, 6 * LANES, 7 * LANES

    def to_x(m):
        core_gram(m).wait_recv()
        gx_send[m - 1] = (g_acc[m, half:quart, :] + g_recv[m, :2 * LANES, :].astype(F32)).astype(BF16)
        x_gram(m).start()
        g_acc[m, quart:, :] += g_recv[m, 2 * LANES:, :].astype(F32)

    def to_y(m):
        x_gram(m).wait_recv()
        gy_send[m - 1] = (g_acc[m, quart:eighth, :] + gx_recv[m - 1, :LANES, :].astype(F32)).astype(BF16)
        y_gram(m).start()
        g_acc[m, eighth:, :] += gx_recv[m - 1, LANES:, :].astype(F32)

    def to_z(m):
        y_gram(m).wait_recv()
        full = g_acc[m, eighth:, :] + gy_recv[m - 1].astype(F32)
        gz_send[m - 1] = full.astype(BF16)
        for j in range(1, nz):
            z_copy(m, j).start()
        gm_send[m - 1] = full.T.astype(BF16)
        for to in range(nz):
            mirror_copy(m, to).start()
        gz_keep[m - 1] = full

    def ends_to_z(e):
        m = ENDS[e]
        core_gram(m).wait_recv()
        full = g_acc[m, half:, :] + g_recv[m].astype(F32)
        narrow = full.astype(BF16)
        for k in range(4):
            for zz in range(nz):
                first = k * LANES + zz * out_rows
                ez_send[e, zz, k * out_rows:(k + 1) * out_rows, :] = narrow[first:first + out_rows, :]
        for j in range(1, nz):
            ends_z(e, j).start()
        g_acc[m, half:, :] = full

    def ends_to_plane(e):
        landed(ez_recv.at[e], ez_rsem.at[e])
        for k in range(4):
            first = pl.multiple_of(half + k * LANES + z * out_rows, out_rows)
            acc = g_acc[ENDS[e], pl.ds(first, out_rows), :]
            for j in range(1, nz):
                acc = acc + ez_recv[e, j - 1, k * out_rows:(k + 1) * out_rows, :].astype(F32)
            if k < 3:
                ep_send[e, k] = acc.astype(BF16)
                ends_p(e, k).start()
            else:
                e_keep[e] = acc

    final = source_plane(nz - 1) * GROUP
    gather(final + x_bit, 1)
    final = final + 1 - x_bit
    weigh(final, 1)
    s_send[1] += partial_sums(final, 1, 1, 1 - c_bit)
    core_sums(1).start()
    residual(final, 1)
    for k in range(4):
        new = gram_band(k, 1)
        for m in range(TILES):
            at = slice(k * LANES, (k + 1) * LANES)
            g_send[m, at, :] = (g_acc[m, at, :] + new[:, m * LANES:(m + 1) * LANES]).astype(BF16)
    for m in (1, ENDS[0], 2, ENDS[1], 3):
        core_gram(m).start()
    s_keep[1] += partial_sums(final, 1, 1, c_bit)
    core_sums(1).wait_recv()
    s_send2[...] = (s_keep[1] + s_recv[1]).astype(BF16)
    y_sums(0, 2).start()
    for k in range(4, 8):
        add_gram(k, 1)
    to_x(1)
    ends_to_z(0)
    to_x(2)
    ends_to_z(1)
    to_x(3)
    s_send[0] += partial_sums(final, 1, 0, 1 - c_bit)
    core_sums(0).start()
    mass_send[...] = mass_ref[:1, :]
    masses[q] = mass_ref[:1, :]
    for j in range(1, na):
        mass_copy(lax.rem(q + j, na)).start()
    for b in range(n):
        diag_send[b] = diag_ref[:1, b * LANES:(b + 1) * LANES]
    diags[0] = diag_send[d]

    @pl.loop(1, total)
    def _(j):
        diag_copy(j).start()

    s_keep[0] += partial_sums(final, 1, 0, c_bit)
    to_y(1)
    to_y(2)
    to_y(3)
    y_sums(2, 2).start()
    ends_to_plane(0)
    to_z(1)
    to_z(2)
    to_z(3)
    ends_to_plane(1)

    core_sums(0).wait_recv()
    landed(masses.at[pl.ds(0, na - 1)], mass_rsem.at[0])
    landed(s_recv2, ys_rsem.at[0])
    mass = masses[0]
    for a in range(1, na):
        mass = mass + masses[a]
    col = jnp.broadcast_to(mass, (LANES, ents)).T
    for b in range(feats // LANES):
        cols = slice(b * LANES, (b + 1) * LANES)
        full = s_keep[0, :, cols] + s_recv[0, :, cols] + s_recv2[:, cols].astype(F32)
        new_ref[:, cols] = (full + 1.0 * m_ref[q, :, cols].astype(F32)) / (col + 1.0)

    landed(diags.at[pl.ds(1, total - 1)], diag_rsem.at[0])
    diag = jnp.broadcast_to(jnp.sum(diags[...], axis=0), (out_rows, LANES))
    row = lax.broadcasted_iota(jnp.int32, (out_rows, LANES), 0)
    lane = lax.broadcasted_iota(jnp.int32, (out_rows, LANES), 1)
    diag = jnp.sum(jnp.where(lane == row + q * out_rows, diag, 0.0), axis=1, keepdims=True)
    own_rows = pl.ds(pl.multiple_of(z * out_rows, out_rows), out_rows)
    landed(ep_recv, ep_rsem.at[0])
    for e, m in enumerate(ENDS):
        acc = e_keep[e]
        for k in range(3):
            acc = acc + ep_recv[e, k].astype(F32)
        if m == 0:
            acc = jnp.where(lane == row + z * out_rows, diag, acc)
        p_ref[lax.rem(mine + m, 8)] = acc
    landed(gz_recv, gz_rsem.at[0])
    for m in range(1, MIRROR + 1):
        acc = gz_keep[m - 1, own_rows, :]
        for j in range(1, nz):
            acc = acc + gz_recv[j - 1, m - 1].astype(F32)
        p_ref[lax.rem(mine + m, 8)] = acc
    landed(gm_recv, gm_rsem.at[0])
    for m in range(1, MIRROR + 1):
        acc = jnp.zeros((out_rows, LANES), F32)
        for zz in range(nz):
            acc = acc + gm_recv[zz, m - 1].astype(F32)
        p_ref[lax.rem(mine + 8 - m, 8)] = acc
    for b in range(n):
        zz, xx = b // 2, b % 2
        gram_ref[:, b * LANES:(b + 1) * LANES] = jnp.concatenate(
            [
                p_ref[(e % 2) * 4 + xx * 2 + e // 2, :, zz * out_rows:(zz + 1) * out_rows]
                for e in range(na)
            ],
            axis=1,
        ) / float(rec_dev * n)

    landed(m_ref.at[pl.ds(0, na - 1)], mean_send.at[0])
    landed(masses.at[pl.ds(0, na - 1)], mass_ssem.at[0])
    landed(s_send, sum_ssem.at[0])
    landed(s_send2, ys_ssem.at[0])
    landed(diags.at[pl.ds(1, total - 1)], diag_ssem.at[0])
    landed(g_send, gc_ssem.at[0])
    landed(gx_send, gx_ssem.at[0])
    landed(gy_send, gy_ssem.at[0])
    landed(gz_recv, gz_ssem.at[0])
    landed(gm_recv, gm_ssem.at[0])
    landed(ez_recv, ez_ssem.at[0])
    landed(ep_recv, ep_ssem.at[0])
    landed(metas.at[pl.ds(0, n - 1)], meta_send.at[0])
    landed(packed.at[pl.ds(0, (total - 1) * sub), :], rec_send.at[0])

def finish_kernel(means_ref, gram_ref, means_out, gram_out, sems):
    step = means_ref.shape[0] // 4
    copies = [
        pltpu.make_async_copy(
            means_ref.at[pl.ds(c * step, step)], means_out.at[pl.ds(c * step, step)], sems.at[c]
        )
        for c in range(4)
    ] + [pltpu.make_async_copy(gram_ref, gram_out, sems.at[4])]
    for copy in copies:
        copy.start()
    for copy in copies:
        copy.wait()


def fused(n, na, records, owner, entity_means, noise_bits):
    rec_dev, feats = records.shape
    ents = entity_means.shape[0]
    cap = 2 * rec_dev // n
    slots = 2 * rec_dev // na
    rows = GROUP * (cap // na)
    width = feats * na
    total = n * na
    out_rows = width // total
    nz = n // 2
    vm, dma = pltpu.VMEM, pltpu.SemaphoreType.DMA
    vspec = pl.BlockSpec(memory_space=pltpu.VMEM)
    hspec = pl.BlockSpec(memory_space=pl.ANY)
    scratch = [
        vm((1, rec_dev), jnp.int32), vm((rec_dev, feats), BF16),
        vm((1, rec_dev), jnp.int32), vm((n, LANES), jnp.int32), vm((n, n, LANES), jnp.int32),
        vm((n * cap, feats), BF16), vm((na, slots, feats), BF16), vm((na, ents, feats), BF16),
        vm((slots, ents), jnp.int32), vm((slots, ents), F32), vm((rows, LANES), F32), vm((rows, ents), BF16), vm((ents, rows), BF16),
        vm((rows, width), BF16), vm(((8 + TILES - 1) * LANES, rows), BF16),
        vm((8, ents), F32), vm((1, ents), F32), vm((na, 1, ents), F32),
        vm((8, width), F32), vm((n, 1, LANES), F32), vm((total, 1, LANES), F32),
        vm((2, ents, feats), F32), vm((2, ents, feats), F32), vm((2, ents, feats), F32),
        vm((ents, feats), BF16), vm((ents, feats), BF16),
        vm((TILES, 8 * LANES, LANES), F32),
        vm((TILES, 4 * LANES, LANES), BF16), vm((TILES, 4 * LANES, LANES), BF16),
        vm((MIRROR, 2 * LANES, LANES), BF16), vm((MIRROR, 2 * LANES, LANES), BF16),
        vm((MIRROR, LANES, LANES), BF16), vm((MIRROR, LANES, LANES), BF16),
        vm((MIRROR, LANES, LANES), F32), vm((MIRROR, LANES, LANES), BF16),
        vm((nz - 1, MIRROR, out_rows, LANES), BF16),
        vm((MIRROR, LANES, LANES), BF16), vm((nz, MIRROR, out_rows, LANES), BF16),
        vm((2, nz, LANES, LANES), BF16), vm((2, nz - 1, LANES, LANES), BF16),
        vm((2, 3, out_rows, LANES), BF16), vm((2, 3, out_rows, LANES), BF16), vm((2, out_rows, LANES), F32),
        vm((8, out_rows, LANES), F32),
        dma((3,)),
        dma((1,)), dma((n,)), dma((1,)), dma((n,)), *(dma((1,)) for _ in range(7)),
        dma((1,)), dma((2,)), *(dma((size,)) for size in (1, TILES, 1, MIRROR, 1, MIRROR)),
        *(dma((1,)) for _ in range(6)), *(dma((size,)) for size in (1, 2, 1, 1)),
    ]
    new_means, gram = pl.pallas_call(
        functools.partial(sweep_kernel, n, na),
        out_shape=(vm((ents, feats), F32), vm((out_rows, width), F32)),
        in_specs=[hspec, hspec, hspec, hspec],
        out_specs=(vspec, vspec),
        scratch_shapes=scratch,
        compiler_params=pltpu.CompilerParams(
            collective_id=0, has_side_effects=True, vmem_limit_bytes=56 * 1024 * 1024
        ),
    )(owner.reshape(1, rec_dev), records, entity_means, noise_bits)
    return pl.pallas_call(
        finish_kernel,
        out_shape=(jax.ShapeDtypeStruct((ents, feats), F32), jax.ShapeDtypeStruct((out_rows, width), F32)),
        in_specs=[vspec, vspec],
        out_specs=(hspec, hspec),
        scratch_shapes=[dma((5,))],
    )(pltpu.with_memory_space_constraint(new_means, pltpu.VMEM), pltpu.with_memory_space_constraint(gram, pltpu.VMEM))


def sweep(records, owner, entity_means, noise_bits):
    n, na = lax.axis_size("dom"), lax.axis_size("attr")
    rec_dev, feats = records.shape
    sub = 2 * rec_dev // n // na
    out_rows = feats // n
    if na == 4 and n == 8 and sub % 16 == 0 and out_rows == 32:
        return fused(n, na, records, owner, entity_means, noise_bits)
    return shards(records, owner, entity_means, noise_bits)


def solution(mesh):
    in_specs = (P("dom", "attr"), P("dom", None), P("dom", "attr"), P("dom", None))
    out_specs = (P("dom", "attr"), P(("dom", "attr"), None))
    return jax.shard_map(sweep, mesh=mesh, in_specs=in_specs, out_specs=out_specs, check_vma=False)
```

```python
import functools

import jax
import jax.numpy as jnp
from jax import lax
from jax.experimental import pallas as pl
from jax.experimental.pallas import tpu as pltpu
from jax.sharding import PartitionSpec as P


def posterior(raw, bits, live, width):
    uniform = (bits.astype(jnp.float32) + 0.5) / 8192.0
    noise = -jnp.log(-jnp.log(uniform))
    logits = 3.0 * jnp.tanh(raw * width ** (-0.5)) + noise
    expd = jnp.exp(logits)
    return (expd / jnp.sum(expd, axis=1, keepdims=True) * live[:, None]).astype(jnp.bfloat16)


def shards(records, owner, entity_means, noise_bits):
    dom_count = lax.axis_size("dom")
    attr_count = lax.axis_size("attr")
    rec_dev, feat_cols = records.shape
    slot_count = 2 * rec_dev
    capacity = slot_count // dom_count
    width = feat_cols * attr_count
    total_records = rec_dev * dom_count
    dest = owner[:, 0]
    onehot = (dest[:, None] == jnp.arange(dom_count, dtype=jnp.int32)[None, :]).astype(jnp.float32)
    order = jnp.arange(rec_dev, dtype=jnp.int32)
    earlier = (order[:, None] >= order[None, :]).astype(jnp.bfloat16)
    running = jnp.dot(earlier, onehot.astype(jnp.bfloat16), preferred_element_type=jnp.float32)
    rank = jnp.sum(running * onehot, axis=1).astype(jnp.int32) - 1
    position = dest * capacity + rank
    packed = jnp.zeros((slot_count, feat_cols), jnp.bfloat16).at[position].set(records)
    flag_buf = (
        jnp.zeros((slot_count,), jnp.bfloat16).at[position].set(jnp.ones((rec_dev,), jnp.bfloat16))
    )
    arrived, arrived_flags = (
        lax.all_to_all(
            packed.reshape(dom_count, capacity, feat_cols),
            "dom",
            split_axis=0,
            concat_axis=0,
            tiled=True,
        ),
        lax.all_to_all(
            flag_buf.reshape(dom_count, capacity), "dom", split_axis=0, concat_axis=0, tiled=True
        ),
    )
    arrived = arrived.reshape(slot_count, feat_cols)
    live = arrived_flags.reshape(slot_count).astype(jnp.float32)
    raw = lax.psum(jnp.dot(arrived, entity_means.T, preferred_element_type=jnp.float32), "attr")
    weights = posterior(raw, noise_bits, live, width)
    sums_cols = jnp.dot(weights.T, arrived, preferred_element_type=jnp.float32)
    mass_col = jnp.sum(weights.astype(jnp.float32), axis=0)[:, None]
    recon = jnp.dot(weights, entity_means, preferred_element_type=jnp.float32)
    col_resid = ((arrived.astype(jnp.float32) - recon) * live[:, None]).astype(jnp.bfloat16)
    residual = lax.all_to_all(col_resid, "attr", split_axis=0, concat_axis=1, tiled=True)
    new_means = (sums_cols + 1.0 * entity_means.astype(jnp.float32)) / (mass_col + 1.0)
    term = lax.dot_general(
        residual, residual, (((0,), (0,)), ((), ())), preferred_element_type=jnp.float32
    )
    gram = lax.psum_scatter(term / total_records, ("dom", "attr"), scatter_dimension=0, tiled=True)
    return (new_means, gram)

MESH = pl.DeviceIdType.MESH
F32, BF16 = jnp.float32, jnp.bfloat16
GROUP = 2
LANES = 128
TILES = 5
MIRROR = 3
ENDS = (0, 4)


def nt(a, b):
    return lax.dot_general(a, b, (((1,), (1,)), ((), ())), preferred_element_type=F32)


def nn(a, b):
    return jnp.dot(a, b, preferred_element_type=F32)


def remote(src, dst, send_sem, recv_sem, dev):
    return pltpu.make_async_remote_copy(
        src_ref=src, dst_ref=dst, send_sem=send_sem, recv_sem=recv_sem, device_id=dev, device_id_type=MESH
    )


def landed(ref, sem):
    pltpu.make_async_copy(ref, ref, sem).wait()


def sweep_kernel(
    n, na, owner_hbm, records_hbm, means_hbm, noise_ref, new_ref, gram_ref,
    owner_ref, records_ref,
    rank_ref, meta_ref, metas, packed, x_ref, m_ref, bits_ref, gumbel_ref, live_ref, w_ref, wt_ref, r_ref, rt_ref,
    mass_ref, mass_send, masses, diag_ref, diag_send, diags, s_send, s_keep, s_recv, s_send2, s_recv2,
    g_acc, g_send, g_recv, gx_send, gx_recv, gy_send, gy_recv, gz_keep, gz_send, gz_recv, gm_send, gm_recv,
    ez_send, ez_recv, ep_send, ep_recv, e_keep, p_ref,
    in_sem, rec_send, rec_recv, meta_send, meta_recv, mean_send, mean_recv, bits_sem,
    mass_ssem, mass_rsem, diag_ssem, diag_rsem, sum_ssem, sum_rsem, gc_ssem, gc_rsem, gx_ssem, gx_rsem, gy_ssem, gy_rsem,
    gz_ssem, gz_rsem, gm_ssem, gm_rsem, ys_ssem, ys_rsem, ez_ssem, ez_rsem, ep_ssem, ep_rsem,
):
    rec_dev, feats = records_ref.shape
    ents = m_ref.shape[1]
    cap = 2 * rec_dev // n
    sub = cap // na
    width = feats * na
    d, q = lax.axis_index("dom"), lax.axis_index("attr")
    me = d * na + q
    total = n * na
    x_bit, z = lax.rem(d, 2), d // 2
    c_bit, y_bit = lax.rem(q, 2), q // 2
    nz = n // 2
    rows = GROUP * sub
    out_rows = width // total
    inner = lax.rem((z + 1) // 2, 2)

    owner_in = pltpu.make_async_copy(owner_hbm, owner_ref, in_sem.at[0])
    records_in = pltpu.make_async_copy(records_hbm, records_ref, in_sem.at[1])
    means_in = pltpu.make_async_copy(means_hbm, m_ref.at[q], in_sem.at[2])
    owner_in.start()
    records_in.start()
    means_in.start()

    barrier = pltpu.get_barrier_semaphore()

    @pl.loop(1, total)
    def _(i):
        dev = lax.rem(me + i, total)
        pl.semaphore_signal(barrier, inc=1, device_id=(dev // na, lax.rem(dev, na)), device_id_type=MESH)

    def bits_copy(s):
        at = pl.ds(pl.multiple_of(s * cap + q * sub, sub), sub)
        return pltpu.make_async_copy(
            noise_ref.at[at, :], bits_ref.at[pl.ds(pl.multiple_of(s * sub, sub), sub), :], bits_sem.at[0]
        )

    @pl.loop(0, n)
    def _(s):
        bits_copy(s).start()

    owner_in.wait()
    blk = 256
    ids = lax.broadcasted_iota(jnp.int32, (n, blk), 0)
    upper = (
        lax.broadcasted_iota(jnp.int32, (blk, blk), 0) <= lax.broadcasted_iota(jnp.int32, (blk, blk), 1)
    ).astype(F32).astype(BF16)
    cuts = [slice(b * blk, (b + 1) * blk) for b in range(rec_dev // blk)]
    hots = [(ids == owner_ref[:, cols]).astype(F32) for cols in cuts]
    runs = nn(jnp.concatenate(hots, axis=0).astype(BF16), upper)
    carry = jnp.zeros((n, 1), F32)
    for b, cols in enumerate(cuts):
        run = runs[b * n:(b + 1) * n, :] + carry
        rank_ref[:, cols] = (jnp.sum(run * hots[b], axis=0, keepdims=True) - 1.0).astype(jnp.int32)
        carry = carry + jnp.sum(hots[b], axis=1, keepdims=True)
    counts = jnp.broadcast_to(carry, (n, LANES)).astype(jnp.int32)
    meta_ref[...] = counts
    metas[d] = counts

    def plane(i):
        far, across, near = lax.rem(z + 2, nz), nz - 1 - z, z + 1 - 2 * lax.rem(z, 2)
        return jnp.where(i == 0, far, jnp.where(i == 1, across, jnp.where(i == 2, z, near)))

    def target(t):
        return plane(t // 2) * 2 + lax.rem(x_bit + t, 2)

    def source_plane(p):
        outer = jnp.where(p == 0, 1, jnp.where(p == 1, 2, jnp.where(p == 2, 0, 3)))
        return plane(jnp.where(inner == 1, lax.rem(p + 2, nz), outer))

    def mean_copy(peer):
        return remote(m_ref.at[q], m_ref.at[q], mean_send.at[0], mean_recv.at[0], (d, peer))

    def meta_copy(o):
        return remote(meta_ref, metas.at[d], meta_send.at[0], meta_recv.at[d], (o, q))

    def rec_copy(t, j, o):
        return remote(
            packed.at[pl.ds(pl.multiple_of(t * cap + j * sub, sub), sub), :],
            x_ref.at[q, pl.ds(pl.multiple_of(d * sub, sub), sub), :],
            rec_send.at[0], rec_recv.at[d], (o, j),
        )

    def pack(t):
        pos = jnp.where(owner_ref[...] == target(t), rank_ref[...], -1)
        hot = (lax.broadcasted_iota(jnp.int32, (cap, rec_dev), 0) == pos).astype(F32).astype(BF16)
        packed[pl.ds(pl.multiple_of(t * cap, cap), cap), :] = nn(hot, records_ref[...]).astype(BF16)

    def dispatch(t):
        o = target(t)
        for j in range(na):
            mine = jnp.logical_and(o == d, q == j)

            @pl.when(jnp.logical_not(mine))
            def _():
                rec_copy(t, j, o).start()

            @pl.when(mine)
            def _():
                x_ref[j, pl.ds(pl.multiple_of(d * sub, sub), sub), :] = (
                    packed[pl.ds(pl.multiple_of(t * cap + j * sub, sub), sub), :]
                )

        @pl.when(o != d)
        def _():
            meta_copy(o).start()

    records_in.wait()
    pack(0)
    means_in.wait()
    pl.semaphore_wait(barrier, total - 1)
    dispatch(0)
    for j in range(1, na):
        mean_copy(lax.rem(q + j, na)).start()

    @pl.loop(1, n)
    def _(t):
        pack(t)
        dispatch(t)

    core_peer, y_peer = q + 1 - 2 * c_bit, lax.rem(q + 2, na)
    x_peer = d + 1 - 2 * x_bit
    order = [(dc, dx, dy) for dc in (1, 0) for dx in (1, 0) for dy in (1, 0)]
    mine = c_bit * 4 + x_bit * 2 + y_bit

    def flip(bit, by):
        return 1 - bit if by else bit

    mass_ref[...] = jnp.zeros_like(mass_ref)
    diag_ref[...] = jnp.zeros_like(diag_ref)
    s_send[...] = jnp.zeros_like(s_send)
    s_keep[...] = jnp.zeros_like(s_keep)
    g_acc[...] = jnp.zeros_like(g_acc)

    landed(m_ref.at[pl.ds(0, na - 1)], mean_recv.at[0])
    landed(bits_ref, bits_sem.at[0])

    @pl.loop(0, n)
    def _(s):
        at = pl.ds(pl.multiple_of(s * sub, sub), sub)
        gumbel_ref[at, :] = 1.0 / (-jnp.log((bits_ref[at, :].astype(F32) + 0.5) / 8192.0))

    def arrive(s):
        @pl.when(s == d)
        def _():
            landed(packed.at[pl.ds(0, (na - 1) * sub), :], rec_recv.at[s])

        @pl.when(s != d)
        def _():
            landed(metas.at[pl.ds(0, 1)], meta_recv.at[s])
            landed(packed.at[pl.ds(0, na * sub), :], rec_recv.at[s])

    def weigh(first, count):
        size = count * sub
        for t in range(count):
            arrive(first + t)
        at = pl.ds(pl.multiple_of(first * sub, sub), size)
        raw = nt(x_ref[0, at, :], m_ref[0])
        for a in range(1, na):
            raw = raw + nt(x_ref[a, at, :], m_ref[a])
        expd = jnp.exp(3.0 * jnp.tanh(raw * width ** (-0.5))) * gumbel_ref[at, :]
        row = lax.broadcasted_iota(jnp.int32, (size, 1), 0)
        live = jnp.zeros((size, 1), F32)
        for t in range(count):
            cnt = metas[first + t, pl.ds(d, 1), :][:, :1]
            inside = jnp.logical_and(row >= t * sub, row < (t + 1) * sub)
            live = live + jnp.where(jnp.logical_and(inside, row - t * sub + q * sub < cnt), 1.0, 0.0)
        w = (expd * (live / jnp.sum(expd, axis=1, keepdims=True))).astype(BF16)
        w_ref[:size, :] = w
        live_ref[:size, :] = jnp.broadcast_to(live, (size, LANES))
        mass_ref[...] += jnp.broadcast_to(jnp.sum(w.astype(F32), axis=0, keepdims=True), mass_ref.shape)
        for b in range(ents // LANES):
            cols = slice(b * LANES, (b + 1) * LANES)
            wt_ref[cols, :size] = w_ref[:size, cols].T

    def residual(first, count):
        size = count * sub
        at = pl.ds(pl.multiple_of(first * sub, sub), size)
        w, live = w_ref[:size, :], live_ref[:size, :1]
        for a in range(na):
            recon = nn(w, m_ref[a])
            res = ((x_ref[a, at, :].astype(F32) - recon) * live).astype(BF16)
            r_ref[:size, a * feats:(a + 1) * feats] = res
            wide = res.astype(F32)
            square = jnp.sum(wide * wide, axis=0, keepdims=True)
            diag_ref[:, a * feats:(a + 1) * feats] += jnp.broadcast_to(square, (8, feats))
        for b in range(n):
            turned = r_ref[:size, b * LANES:(b + 1) * LANES].T
            zz, xx = b // 2, b % 2
            for e in range(na):
                g = (e % 2) * 4 + xx * 2 + e // 2
                piece = turned[e * out_rows:(e + 1) * out_rows, :]
                for copy in (g, g + 8):
                    if copy < 8 + TILES - 1:
                        rt_ref[pl.ds(copy * LANES + zz * out_rows, out_rows), :size] = piece

    def partial_sums(first, count, t, core):
        at = pl.ds(pl.multiple_of(first * sub, sub), count * sub)
        return nn(wt_ref[:, :count * sub], x_ref[(y_bit if t == 0 else 1 - y_bit) * 2 + core, at, :])

    def band(k):
        dc, dx, dy = order[k]
        return flip(c_bit, dc) * 4 + flip(x_bit, dx) * 2 + flip(y_bit, dy)

    def gram_band(k, count):
        first, size = pl.multiple_of(band(k) * LANES, LANES), count * sub
        return nt(rt_ref[pl.ds(first, LANES), :size], rt_ref[pl.ds(first, TILES * LANES), :size])

    def add_gram(k, count):
        new = gram_band(k, count)
        for m in range(TILES):
            g_acc[m, k * LANES:(k + 1) * LANES, :] += new[:, m * LANES:(m + 1) * LANES]

    def gather(first, count):
        weigh(first, count)
        residual(first, count)
        for t in range(2):
            s_send[t] += partial_sums(first, count, t, 1 - c_bit)
            s_keep[t] += partial_sums(first, count, t, c_bit)
        for k in range(8):
            add_gram(k, count)

    @pl.loop(0, nz - 1)
    def _(p):
        gather(source_plane(p) * GROUP, GROUP)

    def mass_copy(peer):
        return remote(mass_send, masses.at[q], mass_ssem.at[0], mass_rsem.at[0], (d, peer))

    def diag_copy(j):
        dev = lax.rem(me + j, total)
        return remote(
            diag_send.at[dev // na], diags.at[j], diag_ssem.at[0], diag_rsem.at[0], (dev // na, lax.rem(dev, na))
        )

    def core_sums(t):
        return remote(s_send.at[t], s_recv.at[t], sum_ssem.at[0], sum_rsem.at[t], (d, core_peer))

    def y_sums(first, count):
        at = pl.ds(first * LANES, count * LANES)
        return remote(s_send2.at[at], s_recv2.at[at], ys_ssem.at[0], ys_rsem.at[0], (d, y_peer))

    def core_gram(m):
        return remote(g_send.at[m], g_recv.at[m], gc_ssem.at[0], gc_rsem.at[m], (d, core_peer))

    def x_gram(m):
        return remote(gx_send.at[m - 1], gx_recv.at[m - 1], gx_ssem.at[0], gx_rsem.at[m - 1], (x_peer, q))

    def y_gram(m):
        return remote(gy_send.at[m - 1], gy_recv.at[m - 1], gy_ssem.at[0], gy_rsem.at[m - 1], (d, y_peer))

    def z_copy(m, j):
        to = lax.rem(z + j, nz)
        return remote(
            gz_send.at[m - 1, pl.ds(pl.multiple_of(to * out_rows, out_rows), out_rows), :],
            gz_recv.at[j - 1, m - 1], gz_ssem.at[0], gz_rsem.at[0], (to * 2 + x_bit, q),
        )

    def mirror_copy(m, to):
        g = lax.rem(mine + m, 8)
        return remote(
            gm_send.at[m - 1, pl.ds(to * out_rows, out_rows), :],
            gm_recv.at[z, m - 1], gm_ssem.at[0], gm_rsem.at[0],
            (to * 2 + lax.rem(g // 2, 2), lax.rem(g, 2) * 2 + g // 4),
        )

    def ends_z(e, j):
        to = lax.rem(z + j, nz)
        return remote(
            ez_send.at[e, to], ez_recv.at[e, j - 1], ez_ssem.at[0], ez_rsem.at[e], (to * 2 + x_bit, q)
        )

    def ends_p(e, k):
        return remote(
            ep_send.at[e, k], ep_recv.at[e, k], ep_ssem.at[0], ep_rsem.at[0],
            ((x_peer, y_peer), (x_peer, q), (d, y_peer))[k],
        )

    half, quart, eighth = 4 * LANES, 6 * LANES, 7 * LANES

    def to_x(m):
        core_gram(m).wait_recv()
        gx_send[m - 1] = (g_acc[m, half:quart, :] + g_recv[m, :2 * LANES, :].astype(F32)).astype(BF16)
        x_gram(m).start()
        g_acc[m, quart:, :] += g_recv[m, 2 * LANES:, :].astype(F32)

    def to_y(m):
        x_gram(m).wait_recv()
        gy_send[m - 1] = (g_acc[m, quart:eighth, :] + gx_recv[m - 1, :LANES, :].astype(F32)).astype(BF16)
        y_gram(m).start()
        g_acc[m, eighth:, :] += gx_recv[m - 1, LANES:, :].astype(F32)

    def to_z(m):
        y_gram(m).wait_recv()
        full = g_acc[m, eighth:, :] + gy_recv[m - 1].astype(F32)
        gz_send[m - 1] = full.astype(BF16)
        for j in range(1, nz):
            z_copy(m, j).start()
        gm_send[m - 1] = full.T.astype(BF16)
        for to in range(nz):
            mirror_copy(m, to).start()
        gz_keep[m - 1] = full

    def ends_to_z(e):
        m = ENDS[e]
        core_gram(m).wait_recv()
        full = g_acc[m, half:, :] + g_recv[m].astype(F32)
        narrow = full.astype(BF16)
        for k in range(4):
            for zz in range(nz):
                first = k * LANES + zz * out_rows
                ez_send[e, zz, k * out_rows:(k + 1) * out_rows, :] = narrow[first:first + out_rows, :]
        for j in range(1, nz):
            ends_z(e, j).start()
        g_acc[m, half:, :] = full

    def ends_to_plane(e):
        landed(ez_recv.at[e], ez_rsem.at[e])
        for k in range(4):
            first = pl.multiple_of(half + k * LANES + z * out_rows, out_rows)
            acc = g_acc[ENDS[e], pl.ds(first, out_rows), :]
            for j in range(1, nz):
                acc = acc + ez_recv[e, j - 1, k * out_rows:(k + 1) * out_rows, :].astype(F32)
            if k < 3:
                ep_send[e, k] = acc.astype(BF16)
                ends_p(e, k).start()
            else:
                e_keep[e] = acc

    final = source_plane(nz - 1) * GROUP
    gather(final + x_bit, 1)
    final = final + 1 - x_bit
    weigh(final, 1)
    s_send[1] += partial_sums(final, 1, 1, 1 - c_bit)
    core_sums(1).start()
    residual(final, 1)
    for k in range(4):
        new = gram_band(k, 1)
        for m in range(TILES):
            at = slice(k * LANES, (k + 1) * LANES)
            g_send[m, at, :] = (g_acc[m, at, :] + new[:, m * LANES:(m + 1) * LANES]).astype(BF16)
    for m in (*ENDS, 1, 2, 3):
        core_gram(m).start()
    s_keep[1] += partial_sums(final, 1, 1, c_bit)
    core_sums(1).wait_recv()
    s_send2[...] = (s_keep[1] + s_recv[1]).astype(BF16)
    y_sums(0, 2).start()
    for k in range(4, 8):
        add_gram(k, 1)
    ends_to_z(0)
    ends_to_z(1)
    to_x(1)
    to_x(2)
    to_x(3)
    s_send[0] += partial_sums(final, 1, 0, 1 - c_bit)
    core_sums(0).start()
    mass_send[...] = mass_ref[:1, :]
    masses[q] = mass_ref[:1, :]
    for j in range(1, na):
        mass_copy(lax.rem(q + j, na)).start()
    for b in range(n):
        diag_send[b] = diag_ref[:1, b * LANES:(b + 1) * LANES]
    diags[0] = diag_send[d]

    @pl.loop(1, total)
    def _(j):
        diag_copy(j).start()

    s_keep[0] += partial_sums(final, 1, 0, c_bit)
    to_y(1)
    to_y(2)
    to_y(3)
    y_sums(2, 2).start()
    ends_to_plane(0)
    to_z(1)
    to_z(2)
    to_z(3)
    ends_to_plane(1)

    core_sums(0).wait_recv()
    landed(masses.at[pl.ds(0, na - 1)], mass_rsem.at[0])
    landed(s_recv2, ys_rsem.at[0])
    mass = masses[0]
    for a in range(1, na):
        mass = mass + masses[a]
    col = jnp.broadcast_to(mass, (LANES, ents)).T
    for b in range(feats // LANES):
        cols = slice(b * LANES, (b + 1) * LANES)
        full = s_keep[0, :, cols] + s_recv[0, :, cols] + s_recv2[:, cols].astype(F32)
        new_ref[:, cols] = (full + 1.0 * m_ref[q, :, cols].astype(F32)) / (col + 1.0)

    landed(diags.at[pl.ds(1, total - 1)], diag_rsem.at[0])
    diag = jnp.broadcast_to(jnp.sum(diags[...], axis=0), (out_rows, LANES))
    row = lax.broadcasted_iota(jnp.int32, (out_rows, LANES), 0)
    lane = lax.broadcasted_iota(jnp.int32, (out_rows, LANES), 1)
    diag = jnp.sum(jnp.where(lane == row + q * out_rows, diag, 0.0), axis=1, keepdims=True)
    own_rows = pl.ds(pl.multiple_of(z * out_rows, out_rows), out_rows)
    landed(ep_recv, ep_rsem.at[0])
    for e, m in enumerate(ENDS):
        acc = e_keep[e]
        for k in range(3):
            acc = acc + ep_recv[e, k].astype(F32)
        if m == 0:
            acc = jnp.where(lane == row + z * out_rows, diag, acc)
        p_ref[lax.rem(mine + m, 8)] = acc
    landed(gz_recv, gz_rsem.at[0])
    for m in range(1, MIRROR + 1):
        acc = gz_keep[m - 1, own_rows, :]
        for j in range(1, nz):
            acc = acc + gz_recv[j - 1, m - 1].astype(F32)
        p_ref[lax.rem(mine + m, 8)] = acc
    landed(gm_recv, gm_rsem.at[0])
    for m in range(1, MIRROR + 1):
        acc = jnp.zeros((out_rows, LANES), F32)
        for zz in range(nz):
            acc = acc + gm_recv[zz, m - 1].astype(F32)
        p_ref[lax.rem(mine + 8 - m, 8)] = acc
    for b in range(n):
        zz, xx = b // 2, b % 2
        gram_ref[:, b * LANES:(b + 1) * LANES] = jnp.concatenate(
            [
                p_ref[(e % 2) * 4 + xx * 2 + e // 2, :, zz * out_rows:(zz + 1) * out_rows]
                for e in range(na)
            ],
            axis=1,
        ) / float(rec_dev * n)

    landed(m_ref.at[pl.ds(0, na - 1)], mean_send.at[0])
    landed(masses.at[pl.ds(0, na - 1)], mass_ssem.at[0])
    landed(s_send, sum_ssem.at[0])
    landed(s_send2, ys_ssem.at[0])
    landed(diags.at[pl.ds(1, total - 1)], diag_ssem.at[0])
    landed(g_send, gc_ssem.at[0])
    landed(gx_send, gx_ssem.at[0])
    landed(gy_send, gy_ssem.at[0])
    landed(gz_recv, gz_ssem.at[0])
    landed(gm_recv, gm_ssem.at[0])
    landed(ez_recv, ez_ssem.at[0])
    landed(ep_recv, ep_ssem.at[0])
    landed(metas.at[pl.ds(0, n - 1)], meta_send.at[0])
    landed(packed.at[pl.ds(0, (total - 1) * sub), :], rec_send.at[0])

def finish_kernel(means_ref, gram_ref, means_out, gram_out, sems):
    step = means_ref.shape[0] // 4
    copies = [
        pltpu.make_async_copy(
            means_ref.at[pl.ds(c * step, step)], means_out.at[pl.ds(c * step, step)], sems.at[c]
        )
        for c in range(4)
    ] + [pltpu.make_async_copy(gram_ref, gram_out, sems.at[4])]
    for copy in copies:
        copy.start()
    for copy in copies:
        copy.wait()


def fused(n, na, records, owner, entity_means, noise_bits):
    rec_dev, feats = records.shape
    ents = entity_means.shape[0]
    cap = 2 * rec_dev // n
    slots = 2 * rec_dev // na
    rows = GROUP * (cap // na)
    width = feats * na
    total = n * na
    out_rows = width // total
    nz = n // 2
    vm, dma = pltpu.VMEM, pltpu.SemaphoreType.DMA
    vspec = pl.BlockSpec(memory_space=pltpu.VMEM)
    hspec = pl.BlockSpec(memory_space=pl.ANY)
    scratch = [
        vm((1, rec_dev), jnp.int32), vm((rec_dev, feats), BF16),
        vm((1, rec_dev), jnp.int32), vm((n, LANES), jnp.int32), vm((n, n, LANES), jnp.int32),
        vm((n * cap, feats), BF16), vm((na, slots, feats), BF16), vm((na, ents, feats), BF16),
        vm((slots, ents), jnp.int32), vm((slots, ents), F32), vm((rows, LANES), F32), vm((rows, ents), BF16), vm((ents, rows), BF16),
        vm((rows, width), BF16), vm(((8 + TILES - 1) * LANES, rows), BF16),
        vm((8, ents), F32), vm((1, ents), F32), vm((na, 1, ents), F32),
        vm((8, width), F32), vm((n, 1, LANES), F32), vm((total, 1, LANES), F32),
        vm((2, ents, feats), F32), vm((2, ents, feats), F32), vm((2, ents, feats), F32),
        vm((ents, feats), BF16), vm((ents, feats), BF16),
        vm((TILES, 8 * LANES, LANES), F32),
        vm((TILES, 4 * LANES, LANES), BF16), vm((TILES, 4 * LANES, LANES), BF16),
        vm((MIRROR, 2 * LANES, LANES), BF16), vm((MIRROR, 2 * LANES, LANES), BF16),
        vm((MIRROR, LANES, LANES), BF16), vm((MIRROR, LANES, LANES), BF16),
        vm((MIRROR, LANES, LANES), F32), vm((MIRROR, LANES, LANES), BF16),
        vm((nz - 1, MIRROR, out_rows, LANES), BF16),
        vm((MIRROR, LANES, LANES), BF16), vm((nz, MIRROR, out_rows, LANES), BF16),
        vm((2, nz, LANES, LANES), BF16), vm((2, nz - 1, LANES, LANES), BF16),
        vm((2, 3, out_rows, LANES), BF16), vm((2, 3, out_rows, LANES), BF16), vm((2, out_rows, LANES), F32),
        vm((8, out_rows, LANES), F32),
        dma((3,)),
        dma((1,)), dma((n,)), dma((1,)), dma((n,)), *(dma((1,)) for _ in range(7)),
        dma((1,)), dma((2,)), *(dma((size,)) for size in (1, TILES, 1, MIRROR, 1, MIRROR)),
        *(dma((1,)) for _ in range(6)), *(dma((size,)) for size in (1, 2, 1, 1)),
    ]
    new_means, gram = pl.pallas_call(
        functools.partial(sweep_kernel, n, na),
        out_shape=(vm((ents, feats), F32), vm((out_rows, width), F32)),
        in_specs=[hspec, hspec, hspec, hspec],
        out_specs=(vspec, vspec),
        scratch_shapes=scratch,
        compiler_params=pltpu.CompilerParams(
            collective_id=0, has_side_effects=True, vmem_limit_bytes=56 * 1024 * 1024
        ),
    )(owner.reshape(1, rec_dev), records, entity_means, noise_bits)
    return pl.pallas_call(
        finish_kernel,
        out_shape=(jax.ShapeDtypeStruct((ents, feats), F32), jax.ShapeDtypeStruct((out_rows, width), F32)),
        in_specs=[vspec, vspec],
        out_specs=(hspec, hspec),
        scratch_shapes=[dma((5,))],
    )(pltpu.with_memory_space_constraint(new_means, pltpu.VMEM), pltpu.with_memory_space_constraint(gram, pltpu.VMEM))


def sweep(records, owner, entity_means, noise_bits):
    n, na = lax.axis_size("dom"), lax.axis_size("attr")
    rec_dev, feats = records.shape
    sub = 2 * rec_dev // n // na
    out_rows = feats // n
    if na == 4 and n == 8 and sub % 16 == 0 and out_rows == 32:
        return fused(n, na, records, owner, entity_means, noise_bits)
    return shards(records, owner, entity_means, noise_bits)


def solution(mesh):
    in_specs = (P("dom", "attr"), P("dom", None), P("dom", "attr"), P("dom", None))
    out_specs = (P("dom", "attr"), P(("dom", "attr"), None))
    return jax.shard_map(sweep, mesh=mesh, in_specs=in_specs, out_specs=out_specs, check_vma=False)
```
